32 devices in a mesh: node: 8 (over z, x), local: 4 (over y, core).
Axes of the slice: x: 2, y: 2, z: 4, core: 2. Of those that a mesh axis runs over, the one named last changes fastest.
Arguments:
- tokens: bfloat16 [4096, 2048], P(('node', 'local')), may hold values from -6 to 6
- expert_ids: int32 [4096, 6], P(('node', 'local')), may hold values from 0 to 15, all different within a row; in each aligned block of 128 rows (0 to 127, 128 to 255, ...) at most 82 rows name the same one
- gate_codes: int32 [4096, 6], P(('node', 'local')), may hold values from 1 to 1023
- gate_halves: bfloat16 [32, 2048, 704], P(('node', 'local')), may hold values from -0.125 to 0.125
- up_halves: bfloat16 [32, 2048, 704], P(('node', 'local')), may hold values from -0.125 to 0.125
- down_halves: bfloat16 [32, 1408, 1024], P(('node', 'local')), may hold values from -0.15625 to 0.15625
- shared_gate: bfloat16 [2048, 2816], P(None, 'local'), may hold values from -0.125 to 0.125
- shared_up: bfloat16 [2048, 2816], P(None, 'local'), may hold values from -0.125 to 0.125
- shared_down: bfloat16 [2816, 2048], P('local'), may hold values from -0.109375 to 0.109375
Outputs:
- mixed: bfloat16 [4096, 2048], P(('node', 'local'))
The draws below stay inside these ranges and needn't reach their ends.
Inputs may be any that keep to these rules, and one draw needn't show every extreme that they name: `expert_ids`: the experts of one token differ. Among the rows of one device, no expert is named more than 82 times, a bound that some block reaches; every expert is named somewhere.
All inputs are finite; a program needn't handle non-finite values.
Results may differ from the reference program's by a relative error of at most 0.01.
Values may be sent and summed in bfloat16 or wider, within the bound.
A program may use at most 128 MiB of HBM per device.

```python
import math
import jax
import jax.numpy as jnp
import numpy as np
from jax import lax

D = 2048
FF = 1408
SHARED = 2816
TOPK = 6
TOK_DEV = 128
EXPERTS = 16
CAP = 82
TOKENS = 4096
N_LOCAL = 4
DEVICES = 32


def with_ends(entries, stream_key, least, top_value):
    shape = entries.shape
    index_at = [jax.random.randint(jax.random.fold_in(stream_key, axis), (), 0, shape[axis]) for axis in range(len(shape))]
    entries = entries.at[tuple(index_at)].set(least)
    longest = shape.index(max(shape))
    index_at[longest] = (index_at[longest] + 1) % shape[longest]
    return entries.at[tuple(index_at)].set(top_value)


def block_levels(key, shape, cuts, smallest, largest):
    gain, own = 1.0, jax.random.fold_in(key, 6)
    for axis_at, blocks in cuts:
        steps = jnp.exp(jax.random.uniform(jax.random.fold_in(own, axis_at), (blocks,), jnp.float32, smallest / len(cuts), largest / len(cuts)))
        gain = gain * jnp.repeat(steps, shape[axis_at] // blocks).reshape([-1 if axis == axis_at else 1 for axis in range(len(shape))])
    return gain


def routed_block(stream_key, own, number, rows, count, top, limit, slope):
    order = jax.random.permutation(stream_key, count)
    heavy_load, common = portions_of(count, rows * top, limit, slope, True), portions_of(count, rows * top, limit, slope, False)
    places = jnp.arange(count)

    def named(tallies, rotation):
        used = int((tallies > 0).sum())
        fixed = max(1, used // 4)
        shifted = fixed + (places - fixed + rotation * (used - fixed)) % max(1, count - fixed)
        return jnp.zeros((count,), jnp.int32).at[order[jnp.where(places < fixed, places, shifted)]].set(jnp.asarray(tallies, jnp.int32))

    tallies = jnp.where(number % 4 == 0, named(heavy_load, number // 4), named(common, number - number // 4 - 1))
    mixed = jax.random.permutation(jax.random.fold_in(own, 3), count)
    source_of, taker = mixed[0:count // 2 * 2:2], mixed[1:count // 2 * 2:2]
    margin = jnp.minimum(tallies[source_of] - 1, limit - tallies[taker]) // 2
    margin = jnp.where((source_of == order[0]) | (taker == order[0]) | (tallies[taker] == 0), 0, jnp.maximum(margin, 0))
    shifted = jax.random.randint(jax.random.fold_in(own, 4), (count // 2,), 0, 1 << 20) % (margin + 1)
    tallies = tallies.at[source_of].add(-shifted).at[taker].add(shifted)
    labels = jnp.searchsorted(jnp.cumsum(tallies), jnp.arange(rows * top), side="right").astype(jnp.int32)
    listing = labels.reshape(top, rows).T
    listing = listing[jax.random.permutation(jax.random.fold_in(own, 1), rows)]
    rotation = jax.random.randint(jax.random.fold_in(own, 2), (rows, 1), 0, top)
    return jnp.take_along_axis(listing, (jnp.arange(top)[None, :] + rotation) % top, axis=1)


def portions_of(number_of, total, reach, lean, full):
    loads = [(1 << 20) // math.isqrt(standing ** lean) + 1 for standing in range(1, number_of + 1)]
    largest = reach if full else min(reach, max(-(-total // number_of), total * loads[0] // sum(loads)))
    least = 1 if total - largest >= number_of - 1 else 0
    holding, surplus = [largest] + [least] * (number_of - 1), total - largest - least * (number_of - 1)
    while surplus > 0:
        free = [i for i in range(1, number_of) if holding[i] < largest] or [i for i in range(1, number_of) if holding[i] < reach]
        pool, remaining = sum([loads[i] for i in free]), surplus
        for i in free:
            more = min(reach - holding[i], max(1, remaining * loads[i] // pool), surplus)
            holding[i] = holding[i] + more
            surplus = surplus - more
    return np.array(holding)


def gaussian(rng, shape, deviation, reach, split=(), kind=jnp.bfloat16):
    values = deviation * jax.random.normal(rng, shape, jnp.float32)
    if split:
        values = values * block_levels(rng, shape, split, -0.22, 0.18)
    return jnp.clip(values, -reach, reach).astype(kind)


def setup_inputs(seed: int = 0) -> dict:
    key_list = jax.random.split(jax.random.key(seed), 10)
    tokens = gaussian(key_list[0], (TOKENS, D), 1.0, 6.0, ((0, 32),))
    expert_ids_keys = jax.random.split(jax.random.fold_in(key_list[1], 1), TOKENS // TOK_DEV)
    expert_ids_turns = jax.random.permutation(jax.random.fold_in(key_list[1], 3), TOKENS // TOK_DEV)
    expert_ids = jax.vmap(lambda own, number: routed_block(jax.random.fold_in(key_list[1], 2), own, number, TOK_DEV, EXPERTS, TOPK, CAP, 2))(expert_ids_keys, expert_ids_turns).reshape((TOKENS, TOPK))
    gate_codes = with_ends(jax.random.randint(key_list[2], (TOKENS, TOPK), 1, 1024), jax.random.fold_in(key_list[2], 1), 1, 1023).astype(jnp.int32)
    gate_halves = gaussian(key_list[3], (2 * EXPERTS, D, FF // 2), D ** -0.5, 0.125, ((0, 32),))
    up_halves = gaussian(key_list[4], (2 * EXPERTS, D, FF // 2), D ** -0.5, 0.125, ((0, 32),))
    down_halves = gaussian(key_list[5], (2 * EXPERTS, FF, D // 2), FF ** -0.5, 0.15625, ((0, 32),))
    shared_gate = gaussian(key_list[6], (D, SHARED), D ** -0.5, 0.125, ((1, 4),))
    shared_up = gaussian(key_list[7], (D, SHARED), D ** -0.5, 0.125, ((1, 4),))
    shared_down = gaussian(key_list[8], (SHARED, D), SHARED ** -0.5, 0.109375, ((0, 4),))
    return {"tokens": tokens, "expert_ids": expert_ids, "gate_codes": gate_codes, "gate_halves": gate_halves, "up_halves": up_halves, "down_halves": down_halves, "shared_gate": shared_gate, "shared_up": shared_up, "shared_down": shared_down}


def reference(tokens, expert_ids, gate_codes, gate_halves, up_halves, down_halves, shared_gate, shared_up, shared_down):
    features = tokens.shape[1]
    route_ids = expert_ids.reshape(DEVICES, TOK_DEV * TOPK).astype(jnp.int32)
    onehot = (route_ids[:, :, None] == jnp.arange(EXPERTS, dtype=jnp.int32)[None, None, :]).astype(jnp.int32)
    slot_index = jnp.sum((jnp.cumsum(onehot, axis=1) - 1) * onehot, axis=2).astype(jnp.int32)
    source_rows = jnp.arange(DEVICES, dtype=jnp.int32)[:, None]
    slot_column = (source_rows * CAP + slot_index).astype(jnp.int32)
    owner_row = (jnp.arange(DEVICES * TOK_DEV * TOPK, dtype=jnp.int32) // TOPK).astype(jnp.int32).reshape(DEVICES, TOK_DEV * TOPK)
    codes = gate_codes.astype(jnp.float32)
    weights = (codes / jnp.sum(codes, axis=1, keepdims=True)).reshape(DEVICES, TOK_DEV * TOPK)
    token_table = jnp.full((EXPERTS, DEVICES * CAP), TOKENS, jnp.int32).at[route_ids, slot_column].set(owner_row)
    weight_table = jnp.zeros((EXPERTS, DEVICES * CAP), jnp.float32).at[route_ids, slot_column].set(weights)
    padded = jnp.concatenate([tokens, jnp.zeros((1, features), tokens.dtype)], axis=0)

    def add_expert(running, expert):
        rows_index = token_table[expert]
        expert_rows = padded[rows_index]
        gate_full = jnp.concatenate([gate_halves[2 * expert], gate_halves[2 * expert + 1]], axis=1)
        up_full = jnp.concatenate([up_halves[2 * expert], up_halves[2 * expert + 1]], axis=1)
        down_full = jnp.concatenate([down_halves[2 * expert], down_halves[2 * expert + 1]], axis=1)
        gate_out = jnp.dot(expert_rows, gate_full, preferred_element_type=jnp.float32)
        up_out = jnp.dot(expert_rows, up_full, preferred_element_type=jnp.float32)
        hidden = (jax.nn.silu(gate_out) * up_out).astype(tokens.dtype)
        result = jnp.dot(hidden, down_full, preferred_element_type=jnp.float32).astype(tokens.dtype)
        running = running.at[rows_index].add(result.astype(jnp.float32) * weight_table[expert][:, None])
        return running, None

    routed, unused = lax.scan(add_expert, jnp.zeros((TOKENS + 1, features), jnp.float32), jnp.arange(EXPERTS, dtype=jnp.int32))
    shared_hidden = (jax.nn.silu(jnp.dot(tokens, shared_gate, preferred_element_type=jnp.float32)) * jnp.dot(tokens, shared_up, preferred_element_type=jnp.float32)).astype(tokens.dtype)
    slice_width = SHARED // N_LOCAL
    shared_out = jnp.zeros((TOKENS, features), jnp.float32)
    for column in range(N_LOCAL):
        partial_sum = jnp.dot(shared_hidden[:, column * slice_width:(column + 1) * slice_width], shared_down[column * slice_width:(column + 1) * slice_width], preferred_element_type=jnp.float32)
        shared_out = shared_out + partial_sum.astype(tokens.dtype).astype(jnp.float32)
    return (routed[:TOKENS] + shared_out).astype(tokens.dtype)
```

```python
import functools

import jax
import jax.numpy as jnp
from jax import lax
from jax.experimental import pallas as pl
from jax.experimental.pallas import tpu as pltpu
from jax.sharding import PartitionSpec as P

MESH = pl.DeviceIdType.MESH
NT = (((1,), (1,)), ((), ()))


def from_partner(block, axis, distance):
    count = lax.axis_size(axis)
    route = []
    for low in range(count):
        high = low | 1 << distance
        if high != low and high < count:
            route += [(low, high), (high, low)]
    return lax.ppermute(block, axis, route)


def dispatch(send_block):
    return lax.all_to_all(send_block, ("node", "local"), split_axis=0, concat_axis=0, tiled=True)


def combine(send_block):
    return lax.all_to_all(send_block, ("node", "local"), split_axis=0, concat_axis=0, tiled=True)


def half_hidden(received, gate_half, up_half, dtype):
    expert_rows = received.reshape(-1, received.shape[-1])
    gate_out = jnp.dot(expert_rows, gate_half, preferred_element_type=jnp.float32)
    up_out = jnp.dot(expert_rows, up_half, preferred_element_type=jnp.float32)
    return (jax.nn.silu(gate_out) * up_out).astype(dtype)


def side_by_side(own_part, other_part, parity, axis):
    lower = jnp.where(parity == 0, own_part, other_part)
    upper = jnp.where(parity == 0, other_part, own_part)
    return jnp.concatenate([lower, upper], axis=axis)


def local(
    tokens,
    expert_ids,
    gate_codes,
    gate_halves,
    up_halves,
    down_halves,
    shared_gate,
    shared_up,
    shared_down,
):
    tok_rows, features = tokens.shape
    fanout = expert_ids.shape[1]
    devices = lax.axis_size("node") * lax.axis_size("local")
    experts = devices // 2
    capacity = 2 * (5 * tok_rows * fanout // (6 * experts) + 1)
    parity = lax.axis_index("local") % 2
    flat_ids = expert_ids.reshape(-1)
    onehot = (flat_ids[:, None] == jnp.arange(experts, dtype=jnp.int32)[None, :]).astype(jnp.int32)
    order = jnp.arange(flat_ids.shape[0], dtype=jnp.int32)
    earlier = (order[:, None] > order[None, :]).astype(jnp.bfloat16)
    before = jnp.dot(earlier, onehot.astype(jnp.bfloat16), preferred_element_type=jnp.float32)
    slot_index = jnp.sum(before.astype(jnp.int32) * onehot, axis=1)
    dest_row = flat_ids * capacity + slot_index
    owner_row = jnp.arange(tok_rows * fanout, dtype=jnp.int32) // fanout
    buffer = (
        jnp.zeros((experts * capacity, features), tokens.dtype).at[dest_row].set(tokens[owner_row])
    )
    codes = gate_codes.astype(jnp.float32)
    weights = (codes / jnp.sum(codes, axis=1, keepdims=True)).reshape(-1)
    send_block = jnp.broadcast_to(
        buffer.reshape(experts, 1, capacity, features), (experts, 2, capacity, features)
    ).reshape(devices, capacity, features)
    received = dispatch(send_block)
    hidden_own = half_hidden(received, gate_halves[0], up_halves[0], tokens.dtype)
    hidden_other = from_partner(hidden_own, "local", 0)
    hidden = side_by_side(hidden_own, hidden_other, parity, 1)
    result = jnp.dot(hidden, down_halves[0], preferred_element_type=jnp.float32).astype(
        tokens.dtype
    )
    returned = combine(result.reshape(devices, capacity, features // 2))
    outputs = (
        returned.reshape(experts, 2, capacity, features // 2)
        .transpose(0, 2, 1, 3)
        .reshape(experts * capacity, features)
    )
    picked = outputs[dest_row].astype(jnp.float32) * weights[:, None]
    routed = jnp.sum(picked.reshape(tok_rows, fanout, features), axis=1)
    block_rows = lax.all_gather(tokens, "local", axis=0, tiled=True)
    gate_part = jnp.dot(block_rows, shared_gate, preferred_element_type=jnp.float32)
    up_part = jnp.dot(block_rows, shared_up, preferred_element_type=jnp.float32)
    shared_hidden = (jax.nn.silu(gate_part) * up_part).astype(tokens.dtype)
    block_rows = shared_hidden
    shared_out = lax.psum_scatter(
        jnp.dot(block_rows, shared_down, preferred_element_type=jnp.float32).astype(jnp.bfloat16),
        "local",
        scatter_dimension=0,
        tiled=True,
    ).astype(jnp.float32)
    return (routed + shared_out).astype(tokens.dtype)


LINE = 4


def layer_kernel(cut, *refs):
    tokens, ids, codes, gate, up, down, s_gate, s_up, s_down, out = refs[:10]
    held, from_q, from_p, from_z, from_b = refs[10:15]
    w_gate, w_up, w_down, v_gate, v_up, v_down = refs[15:21]
    share_out, share_in, pair_in, pair_out, pair_back, extra = refs[21:27]
    load_sem, swap_send, swap_recv, pair_send, pair_recv = refs[27:32]
    share_send, share_recv, send_sem, recv_sem = refs[32:]
    rows, features = tokens.shape
    node, y, core = lax.axis_index("node"), lax.axis_index("chip"), lax.axis_index("core")
    z, x = node // 2, node % 2
    upper = z // 2
    planes = [z, z + 1 - 2 * (z % 2), 2 - upper, 3 - 3 * upper]
    y_side = 2 - core

    def spot(plane, side):
        flip_x = (side % 2) * (1 - core) + (side // 2) * core
        flip_y = (side % 2) * core + (side // 2) * (1 - core)
        return plane, x + flip_x * (1 - 2 * x), y + flip_y * (1 - 2 * y)

    def device(plane, side):
        at_z, at_x, at_y = spot(plane, side)
        return at_z * 2 + at_x, at_y, core

    partner = (node, y, 1 - core)
    p_device, q_device = device(z, 1), device(z, 2)
    others = [(lax.rem(z + d, LINE), side) for d in range(LINE) for side in range(4) if d or side]
    barrier = pltpu.get_barrier_semaphore()
    for target in [device(*other) for other in others] + [partner]:
        pl.semaphore_signal(barrier, inc=1, device_id=target, device_id_type=MESH)
    pl.semaphore_wait(barrier, len(others) + 1)

    Z_WHOLE, Z_REST, P_IN, Q_IN, Q_BACK, P_BACK, Z_BACK, Z_MORE = (4 * k for k in range(8))
    Q_FAR, Q_BACK_FAR = 32, 36
    sent = []

    def copy_of(source, target, at, number, to):
        return pltpu.make_async_remote_copy(
            src_ref=source,
            dst_ref=target,
            send_sem=send_sem.at[number],
            recv_sem=recv_sem.at[at],
            device_id=to,
            device_id_type=MESH,
        )

    def push(source, target, at, to, allowed=None):
        copy = copy_of(source, target, at, len(sent), to)
        if allowed is None:
            copy.start()
        else:
            pl.when(allowed)(copy.start)
        sent.append((copy, allowed))
        return len(sent) - 1

    waited = set()

    def left(number):
        if number in waited:
            return
        waited.add(number)
        copy, allowed = sent[number]
        if allowed is None:
            copy.wait_send()
        else:
            pl.when(allowed)(copy.wait_send)

    def arrived(target, at):
        copy_of(target, target, at, 0, q_device).wait_recv()

    def first(ref):
        return ref.at[:, pl.ds(0, cut)]

    def rest(ref):
        return ref.at[:, pl.ds(cut, features - cut)]

    split = cut < features
    leaving = {(i, side): [] for i in range(LINE) for side in (0, 1)}

    def along_z(source, target, at, i, side):
        if i == 0:
            for step in (1, -1):
                to = z + step
                inside = jnp.logical_and(to >= 0, to < LINE)
                to = jnp.clip(to, 0, LINE - 1)
                leaving[i, side].append(push(source, target, at, (to * 2 + x, y, core), inside))
        else:
            to = z + jnp.where(planes[i] < z, 1, -1)
            inside = jnp.logical_and(to >= 0, to < LINE)
            to = jnp.clip(to, 0, LINE - 1)
            leaving[i, side].append(push(source, target, at, (to * 2 + x, y, core), inside))

    for copy_to in ("q", "p"):
        if copy_to == "q":
            leaving[0, 0].append(push(tokens, held.at[z, 2], Q_IN + z, q_device))
        else:
            leaving[0, 0].append(push(tokens, held.at[z, 1], P_IN + z, p_device))
    along_z(tokens, held.at[z, 0], Z_WHOLE + z, 0, 0)

    def to_partner(source, target, at):
        copy = pltpu.make_async_remote_copy(
            src_ref=source,
            dst_ref=target,
            send_sem=pair_send.at[at],
            recv_sem=pair_recv.at[at],
            device_id=partner,
            device_id_type=MESH,
        )
        copy.start()
        return copy

    pair = [to_partner(tokens, pair_in.at[0], 0)]
    swaps = []
    for at, (source, target) in enumerate(((gate, w_gate), (up, w_up), (down, w_down))):
        copy = pltpu.make_async_remote_copy(
            src_ref=source,
            dst_ref=target.at[core],
            send_sem=swap_send.at[at],
            recv_sem=swap_recv.at[at],
            device_id=partner,
            device_id_type=MESH,
        )
        copy.start()
        swaps.append(copy)
    loads = [
        pltpu.make_async_copy(source, target, load_sem.at[at])
        for at, (source, target) in enumerate(
            (
                (tokens, held.at[z, 0]),
                (s_gate, v_gate),
                (s_up, v_up),
                (s_down, v_down),
                (gate, w_gate.at[core]),
                (up, w_up.at[core]),
                (down, w_down.at[core]),
            )
        )
    ]
    for copy in loads:
        copy.start()

    scores = codes[...].astype(jnp.float32)
    scores = scores / jnp.sum(scores, axis=1, keepdims=True)
    lanes = lax.broadcasted_iota(jnp.int32, (rows, 128), 1)
    table = jnp.zeros((rows, 128), jnp.float32)
    for k in range(ids.shape[1]):
        table = table + jnp.where(ids[:, k : k + 1] == lanes, scores[:, k : k + 1], 0.0)
    table = table.T
    for expert in range(4 * LINE):
        share_out[expert] = jnp.broadcast_to(table[expert : expert + 1, :], (8, rows))
    shares = []
    for number, other in enumerate(others):
        at_z, at_x, at_y = spot(*other)
        side = other[1]
        copy = pltpu.make_async_remote_copy(
            src_ref=share_out.at[(at_z * 2 + at_x) * 2 + at_y],
            dst_ref=share_in.at[z, side],
            send_sem=share_send.at[number],
            recv_sem=share_recv.at[z * 4 + side],
            device_id=device(*other),
            device_id_type=MESH,
        )
        copy.start()
        shares.append(copy)
    share_in[z, 0] = share_out[node * 2 + y]

    def factor(plane, side):
        return jnp.broadcast_to(share_in[plane, side, 0:1, :], (rows, rows)).T[:, 0:1]

    def enter(i):
        plane = planes[i]
        block = held.at[plane, 0]
        arrived(block, Z_WHOLE + plane)
        along_z(block, block, Z_WHOLE + plane, i, 0)
        target = held.at[plane, 1]
        leaving[i, 0].append(push(first(block), first(target), P_IN + plane, p_device))
        leaving[i, 0].append(push(block, held.at[plane, 2], Q_IN + plane, q_device))

    def pass_on(i):
        plane = planes[i]
        block = held.at[plane, 1]
        if i == 0 or not split:
            arrived(block, P_IN + plane)
        else:
            arrived(first(block), P_IN + plane)
            arrived(rest(block), Z_REST + plane)
        if split:
            along_z(rest(block), rest(block), Z_REST + plane, i, 1)
        leaving[i, 1].append(push(block, held.at[plane, 3], Q_FAR + plane, q_device))

    def shared(block):
        gate_out = lax.dot_general(block, v_gate[...], NT, preferred_element_type=jnp.float32)
        up_out = lax.dot_general(block, v_up[...], NT, preferred_element_type=jnp.float32)
        hidden = (jax.nn.silu(gate_out) * up_out).astype(block.dtype)
        part = jnp.dot(hidden, v_down[...], preferred_element_type=jnp.float32)
        return part.astype(block.dtype).reshape(extra.shape)

    def add_up(target, sources, columns=slice(None)):
        def step(i, carry):
            at = pl.ds(pl.multiple_of(i * 16, 16), 16)
            total = sources[0][at, columns].astype(jnp.float32)
            for source in sources[1:]:
                total = total + source[at, columns].astype(jnp.float32)
            target[at, columns] = total.astype(target.dtype)
            return carry

        lax.fori_loop(0, rows // 16, step, 0)

    def serve(i, half):
        plane = planes[i]
        sides = slice(2 * half, 2 * half + 2)
        block = held[plane, sides].reshape(2 * rows, features)
        depth = w_gate.shape[0] * w_gate.shape[1]
        w_in = (w_gate[...].reshape(depth, features), w_up[...].reshape(depth, features))
        gate_out = lax.dot_general(block, w_in[0], NT, preferred_element_type=jnp.float32)
        up_out = lax.dot_general(block, w_in[1], NT, preferred_element_type=jnp.float32)
        hidden = (jax.nn.silu(gate_out) * up_out).astype(block.dtype)
        scale = jnp.concatenate([factor(plane, 2 * half), factor(plane, 2 * half + 1)], axis=0)
        width = features // 2
        for part in (0, 1):
            result = jnp.dot(hidden, w_down[part], preferred_element_type=jnp.float32)
            held[plane, sides, :, part * width : (part + 1) * width] = (
                (result * scale).astype(held.dtype).reshape(2, rows, width)
            )

    def outer(i):
        plane = planes[i]
        for side, at in ((2, Q_IN), (3, Q_FAR)):
            if i or side == 3:
                arrived(held.at[plane, side], at + plane)
        serve(i, 1)
        if i == 0:
            @pl.when(core == 0)
            def _():
                add_up(held.at[z, 2], [held.at[z, 2], extra.at[1]])
        push(held.at[plane, 3], from_q.at[plane, 1], Q_BACK_FAR + plane, q_device)
        push(held.at[plane, 2], from_q.at[plane, 0], Q_BACK + plane, q_device)

    def inner(i):
        for side in (0, 1):
            for number in leaving[i, side]:
                left(number)
        serve(i, 0)
        if i == 0:
            add_up(held.at[z, 0], [held.at[z, 0], extra.at[0]])

            @pl.when(core == 1)
            def _():
                add_up(held.at[z, 1], [held.at[z, 1], extra.at[1]])

    def q_sum(i):
        plane = planes[i]
        block = held.at[plane, 1]
        arrived(from_q.at[plane, 1], Q_BACK_FAR + plane)
        if i == 0 and split:
            for d in range(1, LINE):
                came = lax.rem(z + d, LINE)
                arrived(rest(from_b.at[came]), Z_MORE + came)
            add_up(block, [block, from_q.at[plane, 1]], slice(0, cut))
            more = [from_b.at[lax.rem(z + d, LINE)] for d in range(1, LINE)]
            add_up(block, [block, from_q.at[plane, 1]] + more, slice(cut, features))
        else:
            add_up(block, [block, from_q.at[plane, 1]])
        if i == 0 or not split:
            push(block, from_p.at[plane], P_BACK + plane, p_device)
        else:
            push(first(block), first(from_p.at[plane]), P_BACK + plane, p_device)
            push(rest(block), rest(from_b.at[z]), Z_MORE + z, device(plane, 0))

    def p_sum(i):
        plane = planes[i]
        block = held.at[plane, 0]
        arrived(from_q.at[plane, 0], Q_BACK + plane)
        sources = [block, from_q.at[plane, 0]]
        if i == 0:
            arrived(from_p.at[plane], P_BACK + plane)
            for d in range(1, LINE):
                came = lax.rem(z + d, LINE)
                arrived(from_z.at[came], Z_BACK + came)
                sources.append(from_z.at[came])
            add_up(out, sources + [from_p.at[plane]])
            return
        if split:
            arrived(first(from_p.at[plane]), P_BACK + plane)
            add_up(block, sources + [from_p.at[plane]], slice(0, cut))
            add_up(block, sources, slice(cut, features))
        else:
            arrived(from_p.at[plane], P_BACK + plane)
            add_up(block, sources + [from_p.at[plane]])
        push(block, from_z.at[z], Z_BACK + z, device(plane, 0))

    enter(1)
    pass_on(0)
    arrived(held.at[z, 2], Q_IN + z)
    loads[0].wait()
    pair.append(to_partner(held.at[z, y_side], pair_in.at[1], 1))
    for copy in loads[1:4]:
        copy.wait()
    for copy in pair:
        copy.wait_recv()
    pair_out[...] = shared(pair_in[...].reshape(2 * rows, features))
    pair.append(to_partner(pair_out, pair_back, 2))
    enter(2)
    pass_on(1)
    extra[...] = shared(jnp.concatenate([held[z, 0], held[z, y_side]], axis=0))
    enter(3)
    pair[2].wait_recv()

    def combine(i, carry):
        at = pl.ds(pl.multiple_of(i * 16, 16), 16)
        for block in (0, 1):
            total = extra[block, at, :].astype(jnp.float32) + pair_back[block, at, :].astype(jnp.float32)
            extra[block, at, :] = total.astype(extra.dtype)
        return carry

    lax.fori_loop(0, rows // 16, combine, 0)
    for copy in loads[4:]:
        copy.wait()
    for copy in swaps:
        copy.wait_recv()
    for d in range(LINE):
        for side in range(4):
            if d or side:
                plane = lax.rem(z + d, LINE)
                pltpu.make_async_remote_copy(
                    src_ref=share_in.at[plane, side],
                    dst_ref=share_in.at[plane, side],
                    send_sem=share_send.at[0],
                    recv_sem=share_recv.at[plane * 4 + side],
                    device_id=q_device,
                    device_id_type=MESH,
                ).wait_recv()
    outer(1)
    pass_on(2)
    inner(1)
    pass_on(3)
    q_sum(1)
    outer(2)
    p_sum(1)
    inner(2)
    q_sum(2)
    outer(3)
    p_sum(2)
    inner(3)
    q_sum(3)
    for copy in pair:
        copy.wait_send()
    outer(0)
    p_sum(3)
    inner(0)
    q_sum(0)
    p_sum(0)
    for number in range(len(sent)):
        left(number)
    for copy in swaps + shares:
        copy.wait_send()


def dense(
    tokens,
    expert_ids,
    gate_codes,
    gate_halves,
    up_halves,
    down_halves,
    shared_gate,
    shared_up,
    shared_down,
):
    rows, features = tokens.shape
    half_depth = gate_halves.shape[2]
    shared_depth = shared_gate.shape[1]
    depth, width = down_halves.shape[1:]
    kind = tokens.dtype
    inside, outside = pl.BlockSpec(memory_space=pltpu.VMEM), pl.BlockSpec(memory_space=pl.ANY)
    block = (rows, features)
    dma = pltpu.SemaphoreType.DMA
    return pl.pallas_call(
        functools.partial(layer_kernel, CUT),
        out_shape=jax.ShapeDtypeStruct(block, kind),
        in_specs=[inside] * 3 + [outside] * 6,
        out_specs=inside,
        scratch_shapes=[
            pltpu.VMEM((LINE, 4, *block), kind),
            pltpu.VMEM((LINE, 2, *block), kind),
            pltpu.VMEM((LINE, *block), kind),
            pltpu.VMEM((LINE, *block), kind),
            pltpu.VMEM((LINE, *block), kind),
            pltpu.VMEM((2, half_depth, features), kind),
            pltpu.VMEM((2, half_depth, features), kind),
            pltpu.VMEM((2, depth, width), kind),
            pltpu.VMEM((shared_depth, features), kind),
            pltpu.VMEM((shared_depth, features), kind),
            pltpu.VMEM((shared_depth, features), kind),
            pltpu.VMEM((4 * LINE, 8, rows), jnp.float32),
            pltpu.VMEM((LINE, 4, 8, rows), jnp.float32),
            pltpu.VMEM((2, *block), kind),
            pltpu.VMEM((2, *block), kind),
            pltpu.VMEM((2, *block), kind),
            pltpu.VMEM((2, *block), kind),
            dma((7,)),
            dma((3,)),
            dma((3,)),
            dma((3,)),
            dma((3,)),
            dma((4 * LINE - 1,)),
            dma((4 * LINE,)),
            dma((64,)),
            dma((40,)),
        ],
        compiler_params=pltpu.CompilerParams(
            collective_id=0, has_side_effects=True, vmem_limit_bytes=62 << 20
        ),
        cost_estimate=pl.CostEstimate(flops=40 << 30, bytes_accessed=32 << 20, transcendentals=0),
    )(
        tokens,
        expert_ids,
        gate_codes,
        gate_halves[0].T,
        up_halves[0].T,
        down_halves[0],
        shared_gate.T,
        shared_up.T,
        shared_down,
    )


CUT = 2048


def program(mesh, row, pieces, body):
    in_specs = (
        P(row, None),
        P(row, None),
        P(row, None),
        P(row, None, None),
        P(row, None, None),
        P(row, None, None),
        P(None, pieces),
        P(None, pieces),
        P(pieces, None),
    )
    return jax.shard_map(
        body, mesh=mesh, in_specs=in_specs, out_specs=P(row, None), check_vma=False
    )


def solution(mesh):
    fine = jax.sharding.Mesh(
        mesh.devices.reshape(mesh.devices.shape[0], -1, 2), ("node", "chip", "core")
    )

    def run(tokens, expert_ids, *others):
        if mesh.shape["local"] == 4 and mesh.shape["node"] == 2 * LINE:
            whole = program(fine, ("node", "chip", "core"), ("chip", "core"), dense)
        else:
            whole = program(mesh, ("node", "local"), "local", local)
        return whole(tokens, expert_ids, *others)

    return run
```

```python
import functools

import jax
import jax.numpy as jnp
from jax import lax
from jax.experimental import pallas as pl
from jax.experimental.pallas import tpu as pltpu
from jax.sharding import PartitionSpec as P

MESH = pl.DeviceIdType.MESH
NT = (((1,), (1,)), ((), ()))


def from_partner(block, axis, distance):
    count = lax.axis_size(axis)
    route = []
    for low in range(count):
        high = low | 1 << distance
        if high != low and high < count:
            route += [(low, high), (high, low)]
    return lax.ppermute(block, axis, route)


def dispatch(send_block):
    return lax.all_to_all(send_block, ("node", "local"), split_axis=0, concat_axis=0, tiled=True)


def combine(send_block):
    return lax.all_to_all(send_block, ("node", "local"), split_axis=0, concat_axis=0, tiled=True)


def half_hidden(received, gate_half, up_half, dtype):
    expert_rows = received.reshape(-1, received.shape[-1])
    gate_out = jnp.dot(expert_rows, gate_half, preferred_element_type=jnp.float32)
    up_out = jnp.dot(expert_rows, up_half, preferred_element_type=jnp.float32)
    return (jax.nn.silu(gate_out) * up_out).astype(dtype)


def side_by_side(own_part, other_part, parity, axis):
    lower = jnp.where(parity == 0, own_part, other_part)
    upper = jnp.where(parity == 0, other_part, own_part)
    return jnp.concatenate([lower, upper], axis=axis)


def local(
    tokens,
    expert_ids,
    gate_codes,
    gate_halves,
    up_halves,
    down_halves,
    shared_gate,
    shared_up,
    shared_down,
):
    tok_rows, features = tokens.shape
    fanout = expert_ids.shape[1]
    devices = lax.axis_size("node") * lax.axis_size("local")
    experts = devices // 2
    capacity = 2 * (5 * tok_rows * fanout // (6 * experts) + 1)
    parity = lax.axis_index("local") % 2
    flat_ids = expert_ids.reshape(-1)
    onehot = (flat_ids[:, None] == jnp.arange(experts, dtype=jnp.int32)[None, :]).astype(jnp.int32)
    order = jnp.arange(flat_ids.shape[0], dtype=jnp.int32)
    earlier = (order[:, None] > order[None, :]).astype(jnp.bfloat16)
    before = jnp.dot(earlier, onehot.astype(jnp.bfloat16), preferred_element_type=jnp.float32)
    slot_index = jnp.sum(before.astype(jnp.int32) * onehot, axis=1)
    dest_row = flat_ids * capacity + slot_index
    owner_row = jnp.arange(tok_rows * fanout, dtype=jnp.int32) // fanout
    buffer = (
        jnp.zeros((experts * capacity, features), tokens.dtype).at[dest_row].set(tokens[owner_row])
    )
    codes = gate_codes.astype(jnp.float32)
    weights = (codes / jnp.sum(codes, axis=1, keepdims=True)).reshape(-1)
    send_block = jnp.broadcast_to(
        buffer.reshape(experts, 1, capacity, features), (experts, 2, capacity, features)
    ).reshape(devices, capacity, features)
    received = dispatch(send_block)
    hidden_own = half_hidden(received, gate_halves[0], up_halves[0], tokens.dtype)
    hidden_other = from_partner(hidden_own, "local", 0)
    hidden = side_by_side(hidden_own, hidden_other, parity, 1)
    result = jnp.dot(hidden, down_halves[0], preferred_element_type=jnp.float32).astype(
        tokens.dtype
    )
    returned = combine(result.reshape(devices, capacity, features // 2))
    outputs = (
        returned.reshape(experts, 2, capacity, features // 2)
        .transpose(0, 2, 1, 3)
        .reshape(experts * capacity, features)
    )
    picked = outputs[dest_row].astype(jnp.float32) * weights[:, None]
    routed = jnp.sum(picked.reshape(tok_rows, fanout, features), axis=1)
    block_rows = lax.all_gather(tokens, "local", axis=0, tiled=True)
    gate_part = jnp.dot(block_rows, shared_gate, preferred_element_type=jnp.float32)
    up_part = jnp.dot(block_rows, shared_up, preferred_element_type=jnp.float32)
    shared_hidden = (jax.nn.silu(gate_part) * up_part).astype(tokens.dtype)
    block_rows = shared_hidden
    shared_out = lax.psum_scatter(
        jnp.dot(block_rows, shared_down, preferred_element_type=jnp.float32).astype(jnp.bfloat16),
        "local",
        scatter_dimension=0,
        tiled=True,
    ).astype(jnp.float32)
    return (routed + shared_out).astype(tokens.dtype)


LINE = 4


def layer_kernel(cut, *refs):
    tokens, ids, codes, gate, up, down, s_gate, s_up, s_down, out = refs[:10]
    held, inward, outward, back_near, back, from_p, from_z = refs[10:17]
    w_gate, w_up, w_down, v_gate, v_up, v_down = refs[17:23]
    share_out, share_in, pick, worth, pair_in, pair_out, pair_back, extra = refs[23:31]
    load_sem, swap_send, swap_recv, pair_send, pair_recv = refs[31:36]
    share_send, share_recv, send_sem, recv_sem = refs[36:]
    rows, features = tokens.shape
    node, y, core = lax.axis_index("node"), lax.axis_index("chip"), lax.axis_index("core")
    z, x = node // 2, node % 2
    upper = z // 2
    planes = [z, z + 1 - 2 * (z % 2), 2 - upper, 3 - 3 * upper]
    slots = inward.shape[1]
    beside = held.at[LINE * (1 - core) + z * core, core]
    far = held.at[LINE]

    def spot(plane, side):
        flip_x = (side % 2) * (1 - core) + (side // 2) * core
        flip_y = (side % 2) * core + (side // 2) * (1 - core)
        return plane, x + flip_x * (1 - 2 * x), y + flip_y * (1 - 2 * y)

    def device(plane, side):
        at_z, at_x, at_y = spot(plane, side)
        return at_z * 2 + at_x, at_y, core

    partner = (node, y, 1 - core)
    p_device, q_device = device(z, 1), device(z, 2)
    others = [(lax.rem(z + d, LINE), side) for d in range(LINE) for side in range(4) if d or side]
    barrier = pltpu.get_barrier_semaphore()
    for target in [device(*other) for other in others] + [partner]:
        pl.semaphore_signal(barrier, inc=1, device_id=target, device_id_type=MESH)
    pl.semaphore_wait(barrier, len(others) + 1)

    Z_WHOLE, Z_REST, P_IN, Q_IN, Q_BACK, P_BACK, Z_BACK = (LINE * k for k in range(7))
    Q_FAR, Q_BACK_FAR = LINE * 7, LINE * 7 + 1
    sent = []

    def copy_of(source, target, at, number, to):
        return pltpu.make_async_remote_copy(
            src_ref=source,
            dst_ref=target,
            send_sem=send_sem.at[number],
            recv_sem=recv_sem.at[at],
            device_id=to,
            device_id_type=MESH,
        )

    def push(source, target, at, to, allowed=None):
        copy = copy_of(source, target, at, len(sent), to)
        if allowed is None:
            copy.start()
        else:
            pl.when(allowed)(copy.start)
        sent.append((copy, allowed))
        return len(sent) - 1

    waited = set()

    def left(number):
        if number in waited:
            return
        waited.add(number)
        copy, allowed = sent[number]
        if allowed is None:
            copy.wait_send()
        else:
            pl.when(allowed)(copy.wait_send)

    def arrived(target, at):
        copy_of(target, target, at, 0, q_device).wait_recv()

    def first(ref):
        return ref.at[:, pl.ds(0, cut)]

    def rest(ref):
        return ref.at[:, pl.ds(cut, features - cut)]

    leaving = {(i, side): [] for i in range(LINE) for side in (0, 1)}

    def along_z(source, target, at, i, side):
        if i == 0:
            for step in (1, -1):
                to = z + step
                inside = jnp.logical_and(to >= 0, to < LINE)
                to = jnp.clip(to, 0, LINE - 1)
                leaving[i, side].append(push(source, target, at, (to * 2 + x, y, core), inside))
        else:
            to = z + jnp.where(planes[i] < z, 1, -1)
            inside = jnp.logical_and(to >= 0, to < LINE)
            to = jnp.clip(to, 0, LINE - 1)
            leaving[i, side].append(push(source, target, at, (to * 2 + x, y, core), inside))

    push(tokens, far.at[0], Q_IN + z, q_device)
    push(tokens, held.at[z, 1], P_IN + z, p_device)
    along_z(tokens, held.at[z, 0], Z_WHOLE + z, 0, 0)

    def to_partner(source, target, at):
        copy = pltpu.make_async_remote_copy(
            src_ref=source,
            dst_ref=target,
            send_sem=pair_send.at[at],
            recv_sem=pair_recv.at[at],
            device_id=partner,
            device_id_type=MESH,
        )
        copy.start()
        return copy

    pair = [to_partner(tokens, pair_in.at[0], 0)]
    swaps = []
    for at, (source, target) in enumerate(((gate, w_gate), (up, w_up), (down, w_down))):
        copy = pltpu.make_async_remote_copy(
            src_ref=source,
            dst_ref=target.at[core],
            send_sem=swap_send.at[at],
            recv_sem=swap_recv.at[at],
            device_id=partner,
            device_id_type=MESH,
        )
        copy.start()
        swaps.append(copy)
    loads = [
        pltpu.make_async_copy(source, target, load_sem.at[at])
        for at, (source, target) in enumerate(
            (
                (tokens, held.at[z, 0]),
                (s_gate, v_gate),
                (s_up, v_up),
                (s_down, v_down),
                (gate, w_gate.at[core]),
                (up, w_up.at[core]),
                (down, w_down.at[core]),
            )
        )
    ]
    for copy in loads:
        copy.start()

    scores = codes[...].astype(jnp.float32)
    scores = scores / jnp.sum(scores, axis=0, keepdims=True)
    names = lax.broadcasted_iota(jnp.int32, (4 * LINE, rows), 0)
    table = jnp.zeros((4 * LINE, rows), jnp.float32)
    for k in range(ids.shape[0]):
        table = table + jnp.where(ids[k : k + 1, :] == names, scores[k : k + 1, :], 0.0)
    for expert in range(4 * LINE):
        beyond = jnp.where(core == 0, table[expert ^ 1], table[expert ^ 2])
        share_out[expert] = jnp.concatenate(
            [table[expert : expert + 1], jnp.broadcast_to(beyond[None], (7, rows))], axis=0
        )
    shares = []
    for number, other in enumerate(others):
        at_z, at_x, at_y = spot(*other)
        side = other[1]
        copy = pltpu.make_async_remote_copy(
            src_ref=share_out.at[(at_z * 2 + at_x) * 2 + at_y],
            dst_ref=share_in.at[z, side],
            send_sem=share_send.at[number],
            recv_sem=share_recv.at[z * 4 + side],
            device_id=device(*other),
            device_id_type=MESH,
        )
        copy.start()
        shares.append(copy)
    share_in[z, 0] = share_out[node * 2 + y]

    def factor(plane, side):
        return jnp.broadcast_to(share_in[plane, side, 0:1, :], (rows, rows)).T[:, 0:1]

    def choose():
        lists = [jnp.concatenate([share_in[i, s, 1:2, :] for s in (0, 1)], axis=1) for i in range(LINE)]
        lists += [jnp.concatenate([share_in[i, s, 0:1, :] for s in (2, 3)], axis=1) for i in range(LINE)]
        lists = jnp.concatenate(lists, axis=0)
        named = jnp.where(lists > 0, 1.0, 0.0)
        square = (2 * rows, 2 * rows)
        earlier = lax.broadcasted_iota(jnp.int32, square, 0) < lax.broadcasted_iota(jnp.int32, square, 1)
        earlier = jnp.where(earlier, 1.0, 0.0).astype(jnp.bfloat16)
        rank = jnp.dot(named.astype(jnp.bfloat16), earlier, preferred_element_type=jnp.float32)
        rank = jnp.where(lists > 0, rank, -1.0)
        slot = lax.broadcasted_iota(jnp.int32, (slots, 2 * rows), 0).astype(jnp.float32)
        for i in range(LINE):
            pick[i] = jnp.where(rank[i : i + 1] == slot, 1.0, 0.0).astype(pick.dtype)
            j = LINE + i
            weight = jnp.where(rank[j : j + 1] == slot, lists[j : j + 1], 0.0)
            worth[i] = jnp.broadcast_to(jnp.sum(weight, axis=1, keepdims=True), worth.shape[1:])

    def enter(i):
        plane = planes[i]
        block = held.at[plane, 0]
        arrived(block, Z_WHOLE + plane)
        along_z(block, block, Z_WHOLE + plane, i, 0)
        target = held.at[plane, 1]
        leaving[i, 0].append(push(first(block), first(target), P_IN + plane, p_device))

    def pass_on(i):
        plane = planes[i]
        block = held.at[plane, 1]
        if i == 0 or cut == features:
            arrived(block, P_IN + plane)
        else:
            arrived(first(block), P_IN + plane)
            arrived(rest(block), Z_REST + plane)
        if cut < features:
            along_z(rest(block), rest(block), Z_REST + plane, i, 1)
        if i == 0:
            leaving[i, 1].append(push(block, far.at[1], Q_FAR, q_device))
        else:
            both = held[plane].reshape(2 * rows, features)
            chosen = jnp.dot(pick[plane], both, preferred_element_type=jnp.float32)
            outward[plane] = chosen.astype(outward.dtype)
            push(outward.at[plane], inward.at[plane], Q_IN + plane, q_device)

    def shared(block):
        gate_out = lax.dot_general(block, v_gate[...], NT, preferred_element_type=jnp.float32)
        up_out = lax.dot_general(block, v_up[...], NT, preferred_element_type=jnp.float32)
        hidden = (jax.nn.silu(gate_out) * up_out).astype(block.dtype)
        part = jnp.dot(hidden, v_down[...], preferred_element_type=jnp.float32)
        return part.astype(block.dtype).reshape(extra.shape)

    def add_up(target, sources, columns=slice(None)):
        def step(i, carry):
            at = pl.ds(pl.multiple_of(i * 16, 16), 16)
            total = sources[0][at, columns].astype(jnp.float32)
            for source in sources[1:]:
                total = total + source[at, columns].astype(jnp.float32)
            target[at, columns] = total.astype(target.dtype)
            return carry

        lax.fori_loop(0, rows // 16, step, 0)

    def serve(target, scale):
        block = target[...].reshape(-1, features)
        depth = w_gate.shape[0] * w_gate.shape[1]
        w_in = (w_gate[...].reshape(depth, features), w_up[...].reshape(depth, features))
        gate_out = lax.dot_general(block, w_in[0], NT, preferred_element_type=jnp.float32)
        up_out = lax.dot_general(block, w_in[1], NT, preferred_element_type=jnp.float32)
        hidden = (jax.nn.silu(gate_out) * up_out).astype(block.dtype)
        width = features // 2
        for part in (0, 1):
            result = jnp.dot(hidden, w_down[part], preferred_element_type=jnp.float32)
            result = (result * scale).astype(target.dtype)
            target[..., part * width : (part + 1) * width] = result.reshape(*target.shape[:-1], width)

    def outer(i):
        plane = planes[i]
        if i:
            arrived(inward.at[plane], Q_IN + plane)
            serve(inward.at[plane], worth[plane, :, 0:1])
            push(inward.at[plane], back.at[plane], Q_BACK + plane, q_device)
            return
        arrived(far.at[1], Q_FAR)
        serve(far, jnp.concatenate([factor(z, 2), factor(z, 3)], axis=0))

        @pl.when(core == 0)
        def _():
            add_up(far.at[0], [far.at[0], extra.at[1]])

        push(far.at[1], back_near.at[1], Q_BACK_FAR, q_device)
        push(far.at[0], back_near.at[0], Q_BACK + z, q_device)

    def inner(i):
        plane = planes[i]
        for side in (0, 1):
            for number in leaving[i, side]:
                left(number)
        serve(held.at[plane], jnp.concatenate([factor(plane, 0), factor(plane, 1)], axis=0))
        if i == 0:
            add_up(held.at[z, 0], [held.at[z, 0], extra.at[0]])

            @pl.when(core == 1)
            def _():
                add_up(held.at[z, 1], [held.at[z, 1], extra.at[1]])

    def spread(plane, side):
        places = pick[plane, :, side * rows : (side + 1) * rows]
        return lax.dot_general(
            places, back[plane], (((0,), (0,)), ((), ())), preferred_element_type=jnp.float32
        )

    def q_sum(i):
        plane = planes[i]
        block = held.at[plane, 1]
        if i == 0:
            arrived(back_near.at[1], Q_BACK_FAR)
            add_up(block, [block, back_near.at[1]])
        else:
            arrived(back.at[plane], Q_BACK + plane)
            block[...] = (block[...].astype(jnp.float32) + spread(plane, 1)).astype(block.dtype)
        push(block, from_p.at[plane], P_BACK + plane, p_device)

    def p_sum(i):
        plane = planes[i]
        block = held.at[plane, 0]
        if i == 0:
            arrived(back_near.at[0], Q_BACK + z)
            arrived(from_p.at[plane], P_BACK + plane)
            sources = [block, back_near.at[0], from_p.at[plane]]
            for d in range(1, LINE):
                came = lax.rem(z + d, LINE)
                arrived(from_z.at[came], Z_BACK + came)
                sources.append(from_z.at[came])
            add_up(out, sources)
            return
        arrived(from_p.at[plane], P_BACK + plane)
        total = block[...].astype(jnp.float32) + from_p[plane].astype(jnp.float32)
        block[...] = (total + spread(plane, 0)).astype(block.dtype)
        push(block, from_z.at[z], Z_BACK + z, device(plane, 0))

    enter(1)
    pass_on(0)
    for d in range(LINE):
        for side in range(4):
            if d or side:
                plane = lax.rem(z + d, LINE)
                pltpu.make_async_remote_copy(
                    src_ref=share_in.at[plane, side],
                    dst_ref=share_in.at[plane, side],
                    send_sem=share_send.at[0],
                    recv_sem=share_recv.at[plane * 4 + side],
                    device_id=q_device,
                    device_id_type=MESH,
                ).wait_recv()
    choose()
    arrived(far.at[0], Q_IN + z)
    loads[0].wait()
    pair.append(to_partner(beside, pair_in.at[1], 1))
    for copy in loads[1:4]:
        copy.wait()
    for copy in pair:
        copy.wait_recv()
    pair_out[...] = shared(pair_in[...].reshape(2 * rows, features))
    pair.append(to_partner(pair_out, pair_back, 2))
    enter(2)
    pass_on(1)
    extra[...] = shared(jnp.concatenate([held[z, 0], beside[...]], axis=0))
    enter(3)
    pair[2].wait_recv()

    def combine(i, carry):
        at = pl.ds(pl.multiple_of(i * 16, 16), 16)
        for block in (0, 1):
            total = extra[block, at, :].astype(jnp.float32) + pair_back[block, at, :].astype(jnp.float32)
            extra[block, at, :] = total.astype(extra.dtype)
        return carry

    lax.fori_loop(0, rows // 16, combine, 0)
    for copy in loads[4:]:
        copy.wait()
    for copy in swaps:
        copy.wait_recv()
    outer(1)
    pass_on(2)
    inner(1)
    pass_on(3)
    q_sum(1)
    outer(2)
    p_sum(1)
    inner(2)
    q_sum(2)
    outer(3)
    p_sum(2)
    inner(3)
    q_sum(3)
    for copy in pair:
        copy.wait_send()
    outer(0)
    p_sum(3)
    inner(0)
    q_sum(0)
    p_sum(0)
    for number in range(len(sent)):
        left(number)
    for copy in swaps + shares:
        copy.wait_send()


def dense(
    tokens,
    expert_ids,
    gate_codes,
    gate_halves,
    up_halves,
    down_halves,
    shared_gate,
    shared_up,
    shared_down,
):
    rows, features = tokens.shape
    capacity = 2 * (5 * rows * expert_ids.shape[1] // (6 * 4 * LINE) + 1)
    slots = -(-2 * capacity // 16) * 16
    half_depth = gate_halves.shape[2]
    shared_depth = shared_gate.shape[1]
    depth, width = down_halves.shape[1:]
    kind = tokens.dtype
    inside, outside = pl.BlockSpec(memory_space=pltpu.VMEM), pl.BlockSpec(memory_space=pl.ANY)
    block = (rows, features)
    dma = pltpu.SemaphoreType.DMA
    return pl.pallas_call(
        functools.partial(layer_kernel, CUT),
        out_shape=jax.ShapeDtypeStruct(block, kind),
        in_specs=[inside] * 3 + [outside] * 6,
        out_specs=inside,
        scratch_shapes=[
            pltpu.VMEM((LINE + 1, 2, *block), kind),
            pltpu.VMEM((LINE, slots, features), kind),
            pltpu.VMEM((LINE, slots, features), kind),
            pltpu.VMEM((2, *block), kind),
            pltpu.VMEM((LINE, slots, features), kind),
            pltpu.VMEM((LINE, *block), kind),
            pltpu.VMEM((LINE, *block), kind),
            pltpu.VMEM((2, half_depth, features), kind),
            pltpu.VMEM((2, half_depth, features), kind),
            pltpu.VMEM((2, depth, width), kind),
            pltpu.VMEM((shared_depth, features), kind),
            pltpu.VMEM((shared_depth, features), kind),
            pltpu.VMEM((shared_depth, features), kind),
            pltpu.VMEM((4 * LINE, 8, rows), jnp.float32),
            pltpu.VMEM((LINE, 4, 8, rows), jnp.float32),
            pltpu.VMEM((LINE, slots, 2 * rows), kind),
            pltpu.VMEM((LINE, slots, rows), jnp.float32),
            pltpu.VMEM((2, *block), kind),
            pltpu.VMEM((2, *block), kind),
            pltpu.VMEM((2, *block), kind),
            pltpu.VMEM((2, *block), kind),
            dma((7,)),
            dma((3,)),
            dma((3,)),
            dma((3,)),
            dma((3,)),
            dma((4 * LINE - 1,)),
            dma((4 * LINE,)),
            dma((64,)),
            dma((40,)),
        ],
        compiler_params=pltpu.CompilerParams(
            collective_id=0, has_side_effects=True, vmem_limit_bytes=62 << 20
        ),
        cost_estimate=pl.CostEstimate(flops=40 << 30, bytes_accessed=32 << 20, transcendentals=0),
    )(
        tokens,
        expert_ids.T,
        gate_codes.T,
        gate_halves[0].T,
        up_halves[0].T,
        down_halves[0],
        shared_gate.T,
        shared_up.T,
        shared_down,
    )


CUT = 1280


def program(mesh, row, pieces, body):
    in_specs = (
        P(row, None),
        P(row, None),
        P(row, None),
        P(row, None, None),
        P(row, None, None),
        P(row, None, None),
        P(None, pieces),
        P(None, pieces),
        P(pieces, None),
    )
    return jax.shard_map(
        body, mesh=mesh, in_specs=in_specs, out_specs=P(row, None), check_vma=False
    )


def solution(mesh):
    fine = jax.sharding.Mesh(
        mesh.devices.reshape(mesh.devices.shape[0], -1, 2), ("node", "chip", "core")
    )

    def run(tokens, expert_ids, *others):
        if mesh.shape["local"] == 4 and mesh.shape["node"] == 2 * LINE:
            whole = program(fine, ("node", "chip", "core"), ("chip", "core"), dense)
        else:
            whole = program(mesh, ("node", "local"), "local", local)
        return whole(tokens, expert_ids, *others)

    return run
```

```python
import functools

import jax
import jax.numpy as jnp
from jax import lax
from jax.experimental import pallas as pl
from jax.experimental.pallas import tpu as pltpu
from jax.sharding import PartitionSpec as P

MESH = pl.DeviceIdType.MESH
NT = (((1,), (1,)), ((), ()))


def from_partner(block, axis, distance):
    count = lax.axis_size(axis)
    route = []
    for low in range(count):
        high = low | 1 << distance
        if high != low and high < count:
            route += [(low, high), (high, low)]
    return lax.ppermute(block, axis, route)


def dispatch(send_block):
    return lax.all_to_all(send_block, ("node", "local"), split_axis=0, concat_axis=0, tiled=True)


def combine(send_block):
    return lax.all_to_all(send_block, ("node", "local"), split_axis=0, concat_axis=0, tiled=True)


def half_hidden(received, gate_half, up_half, dtype):
    expert_rows = received.reshape(-1, received.shape[-1])
    gate_out = jnp.dot(expert_rows, gate_half, preferred_element_type=jnp.float32)
    up_out = jnp.dot(expert_rows, up_half, preferred_element_type=jnp.float32)
    return (jax.nn.silu(gate_out) * up_out).astype(dtype)


def side_by_side(own_part, other_part, parity, axis):
    lower = jnp.where(parity == 0, own_part, other_part)
    upper = jnp.where(parity == 0, other_part, own_part)
    return jnp.concatenate([lower, upper], axis=axis)


def local(
    tokens,
    expert_ids,
    gate_codes,
    gate_halves,
    up_halves,
    down_halves,
    shared_gate,
    shared_up,
    shared_down,
):
    tok_rows, features = tokens.shape
    fanout = expert_ids.shape[1]
    devices = lax.axis_size("node") * lax.axis_size("local")
    experts = devices // 2
    capacity = 2 * (5 * tok_rows * fanout // (6 * experts) + 1)
    parity = lax.axis_index("local") % 2
    flat_ids = expert_ids.reshape(-1)
    onehot = (flat_ids[:, None] == jnp.arange(experts, dtype=jnp.int32)[None, :]).astype(jnp.int32)
    order = jnp.arange(flat_ids.shape[0], dtype=jnp.int32)
    earlier = (order[:, None] > order[None, :]).astype(jnp.bfloat16)
    before = jnp.dot(earlier, onehot.astype(jnp.bfloat16), preferred_element_type=jnp.float32)
    slot_index = jnp.sum(before.astype(jnp.int32) * onehot, axis=1)
    dest_row = flat_ids * capacity + slot_index
    owner_row = jnp.arange(tok_rows * fanout, dtype=jnp.int32) // fanout
    buffer = (
        jnp.zeros((experts * capacity, features), tokens.dtype).at[dest_row].set(tokens[owner_row])
    )
    codes = gate_codes.astype(jnp.float32)
    weights = (codes / jnp.sum(codes, axis=1, keepdims=True)).reshape(-1)
    send_block = jnp.broadcast_to(
        buffer.reshape(experts, 1, capacity, features), (experts, 2, capacity, features)
    ).reshape(devices, capacity, features)
    received = dispatch(send_block)
    hidden_own = half_hidden(received, gate_halves[0], up_halves[0], tokens.dtype)
    hidden_other = from_partner(hidden_own, "local", 0)
    hidden = side_by_side(hidden_own, hidden_other, parity, 1)
    result = jnp.dot(hidden, down_halves[0], preferred_element_type=jnp.float32).astype(
        tokens.dtype
    )
    returned = combine(result.reshape(devices, capacity, features // 2))
    outputs = (
        returned.reshape(experts, 2, capacity, features // 2)
        .transpose(0, 2, 1, 3)
        .reshape(experts * capacity, features)
    )
    picked = outputs[dest_row].astype(jnp.float32) * weights[:, None]
    routed = jnp.sum(picked.reshape(tok_rows, fanout, features), axis=1)
    block_rows = lax.all_gather(tokens, "local", axis=0, tiled=True)
    gate_part = jnp.dot(block_rows, shared_gate, preferred_element_type=jnp.float32)
    up_part = jnp.dot(block_rows, shared_up, preferred_element_type=jnp.float32)
    shared_hidden = (jax.nn.silu(gate_part) * up_part).astype(tokens.dtype)
    block_rows = shared_hidden
    shared_out = lax.psum_scatter(
        jnp.dot(block_rows, shared_down, preferred_element_type=jnp.float32).astype(jnp.bfloat16),
        "local",
        scatter_dimension=0,
        tiled=True,
    ).astype(jnp.float32)
    return (routed + shared_out).astype(tokens.dtype)


LINE = 4


def layer_kernel(cut, *refs):
    tokens, ids, codes, gate, up, down, s_gate, s_up, s_down, out = refs[:10]
    held, own, inward, outward, back_near, back, from_p, from_z = refs[10:18]
    w_gate, w_up, w_down, v_gate, v_up, v_down = refs[18:24]
    share_out, share_in, pick, worth, pair_in, pair_out, pair_back, extra = refs[24:32]
    load_sem, swap_send, swap_recv, pair_send, pair_recv = refs[32:37]
    share_send, share_recv, send_sem, recv_sem = refs[37:]
    rows, features = tokens.shape
    node, y, core = lax.axis_index("node"), lax.axis_index("chip"), lax.axis_index("core")
    z, x = node // 2, node % 2
    upper = z // 2
    planes = [z, z + 1 - 2 * (z % 2), 2 - upper, 3 - 3 * upper]
    slots = inward.shape[1]
    beside = held.at[LINE * (1 - core) + z * core, core]
    far = held.at[LINE]

    def spot(plane, side):
        flip_x = (side % 2) * (1 - core) + (side // 2) * core
        flip_y = (side % 2) * core + (side // 2) * (1 - core)
        return plane, x + flip_x * (1 - 2 * x), y + flip_y * (1 - 2 * y)

    def device(plane, side):
        at_z, at_x, at_y = spot(plane, side)
        return at_z * 2 + at_x, at_y, core

    partner = (node, y, 1 - core)
    p_device, q_device = device(z, 1), device(z, 2)
    others = [(lax.rem(z + d, LINE), side) for d in range(LINE) for side in range(4) if d or side]
    barrier = pltpu.get_barrier_semaphore()
    for target in [device(*other) for other in others] + [partner]:
        pl.semaphore_signal(barrier, inc=1, device_id=target, device_id_type=MESH)
    pl.semaphore_wait(barrier, len(others) + 1)

    Z_WHOLE, Z_REST, P_IN, Q_IN, Q_BACK, P_BACK, P_MORE, Z_BACK = (LINE * k for k in range(8))
    Z_MORE = Z_BACK + LINE + 2
    Q_FAR, Q_BACK_FAR = Z_MORE + LINE + 2, Z_MORE + LINE + 3
    middle = jnp.logical_and(z > 0, z < LINE - 1)
    outermost = jnp.logical_not(middle)
    sent = []

    def copy_of(source, target, at, number, to):
        return pltpu.make_async_remote_copy(
            src_ref=source,
            dst_ref=target,
            send_sem=send_sem.at[number],
            recv_sem=recv_sem.at[at],
            device_id=to,
            device_id_type=MESH,
        )

    def push(source, target, at, to, allowed=None):
        copy = copy_of(source, target, at, len(sent), to)
        if allowed is None:
            copy.start()
        else:
            pl.when(allowed)(copy.start)
        sent.append((copy, allowed))
        return len(sent) - 1

    waited = set()

    def left(number):
        if number in waited:
            return
        waited.add(number)
        copy, allowed = sent[number]
        if allowed is None:
            copy.wait_send()
        else:
            pl.when(allowed)(copy.wait_send)

    def arrived(target, at):
        copy_of(target, target, at, 0, q_device).wait_recv()

    def first(ref):
        return ref.at[:, pl.ds(0, cut)]

    def rest(ref):
        return ref.at[:, pl.ds(cut, features - cut)]

    leaving = {(i, side): [] for i in range(LINE) for side in (0, 1)}

    def along_z(source, target, at, i, side, only=None):
        if i == 0:
            for step in (1, -1):
                to = z + step
                inside = jnp.logical_and(to >= 0, to < LINE)
                to = jnp.clip(to, 0, LINE - 1)
                leaving[i, side].append(push(source, target, at, (to * 2 + x, y, core), inside))
        else:
            to = z + jnp.where(planes[i] < z, 1, -1)
            inside = jnp.logical_and(to >= 0, to < LINE)
            if only is not None:
                inside = jnp.logical_and(inside, only)
            to = jnp.clip(to, 0, LINE - 1)
            leaving[i, side].append(push(source, target, at, (to * 2 + x, y, core), inside))

    push(tokens, far.at[0], Q_IN + z, q_device)
    push(tokens, held.at[z, 1], P_IN + z, p_device)
    along_z(tokens, held.at[z, 0], Z_WHOLE + z, 0, 0)

    def to_partner(source, target, at):
        copy = pltpu.make_async_remote_copy(
            src_ref=source,
            dst_ref=target,
            send_sem=pair_send.at[at],
            recv_sem=pair_recv.at[at],
            device_id=partner,
            device_id_type=MESH,
        )
        copy.start()
        return copy

    pair = [to_partner(tokens, pair_in.at[0], 0)]
    swaps = []
    for at, (source, target) in enumerate(((gate, w_gate), (up, w_up), (down, w_down))):
        copy = pltpu.make_async_remote_copy(
            src_ref=source,
            dst_ref=target.at[core],
            send_sem=swap_send.at[at],
            recv_sem=swap_recv.at[at],
            device_id=partner,
            device_id_type=MESH,
        )
        copy.start()
        swaps.append(copy)
    loads = [
        pltpu.make_async_copy(source, target, load_sem.at[at])
        for at, (source, target) in enumerate(
            (
                (tokens, held.at[z, 0]),
                (s_gate, v_gate),
                (s_up, v_up),
                (s_down, v_down),
                (gate, w_gate.at[core]),
                (up, w_up.at[core]),
                (down, w_down.at[core]),
            )
        )
    ]
    for copy in loads:
        copy.start()

    scores = codes[...].astype(jnp.float32)
    scores = scores / jnp.sum(scores, axis=0, keepdims=True)
    names = lax.broadcasted_iota(jnp.int32, (4 * LINE, rows), 0)
    table = jnp.zeros((4 * LINE, rows), jnp.float32)
    for k in range(ids.shape[0]):
        table = table + jnp.where(ids[k : k + 1, :] == names, scores[k : k + 1, :], 0.0)
    for expert in range(4 * LINE):
        beyond = jnp.where(core == 0, table[expert ^ 1], table[expert ^ 2])
        share_out[expert] = jnp.concatenate(
            [table[expert : expert + 1], jnp.broadcast_to(beyond[None], (7, rows))], axis=0
        )
    shares = []
    for number, other in enumerate(others):
        at_z, at_x, at_y = spot(*other)
        side = other[1]
        copy = pltpu.make_async_remote_copy(
            src_ref=share_out.at[(at_z * 2 + at_x) * 2 + at_y],
            dst_ref=share_in.at[z, side],
            send_sem=share_send.at[number],
            recv_sem=share_recv.at[z * 4 + side],
            device_id=device(*other),
            device_id_type=MESH,
        )
        copy.start()
        shares.append(copy)
    share_in[z, 0] = share_out[node * 2 + y]

    def factor(plane, side):
        return jnp.broadcast_to(share_in[plane, side, 0:1, :], (rows, rows)).T[:, 0:1]

    def choose():
        lists = [jnp.concatenate([share_in[i, s, 1:2, :] for s in (0, 1)], axis=1) for i in range(LINE)]
        lists += [jnp.concatenate([share_in[i, s, 0:1, :] for s in (2, 3)], axis=1) for i in range(LINE)]
        lists = jnp.concatenate(lists, axis=0)
        named = jnp.where(lists > 0, 1.0, 0.0)
        square = (2 * rows, 2 * rows)
        earlier = lax.broadcasted_iota(jnp.int32, square, 0) < lax.broadcasted_iota(jnp.int32, square, 1)
        earlier = jnp.where(earlier, 1.0, 0.0).astype(jnp.bfloat16)
        rank = jnp.dot(named.astype(jnp.bfloat16), earlier, preferred_element_type=jnp.float32)
        rank = jnp.where(lists > 0, rank, -1.0)
        slot = lax.broadcasted_iota(jnp.int32, (slots, 2 * rows), 0).astype(jnp.float32)
        for i in range(LINE):
            pick[i] = jnp.where(rank[i : i + 1] == slot, 1.0, 0.0).astype(pick.dtype)
            j = LINE + i
            weight = jnp.where(rank[j : j + 1] == slot, lists[j : j + 1], 0.0)
            worth[i] = jnp.broadcast_to(jnp.sum(weight, axis=1, keepdims=True), worth.shape[1:])

    def enter(i, only=None):
        plane = planes[i]
        block = held.at[plane, 0]
        if only is None:
            arrived(block, Z_WHOLE + plane)
        else:
            pl.when(only)(lambda: arrived(block, Z_WHOLE + plane))
        along_z(block, block, Z_WHOLE + plane, i, 0, only)
        target = held.at[plane, 1]
        leaving[i, 0].append(push(first(block), first(target), P_IN + plane, p_device, only))

    def pass_on(i):
        plane = planes[i]
        block = held.at[plane, 1]
        if i == 0 or cut == features:
            arrived(block, P_IN + plane)
        else:
            arrived(first(block), P_IN + plane)
            arrived(rest(block), Z_REST + plane)
        if cut < features:
            along_z(rest(block), rest(block), Z_REST + plane, i, 1)
        if i == 0:
            leaving[i, 1].append(push(block, far.at[1], Q_FAR, q_device))
        else:
            both = held[plane].reshape(2 * rows, features)
            chosen = jnp.dot(pick[plane], both, preferred_element_type=jnp.float32)
            outward[plane] = chosen.astype(outward.dtype)
            push(outward.at[plane], inward.at[plane], Q_IN + plane, q_device)

    def shared(block):
        gate_out = lax.dot_general(block, v_gate[...], NT, preferred_element_type=jnp.float32)
        up_out = lax.dot_general(block, v_up[...], NT, preferred_element_type=jnp.float32)
        hidden = (jax.nn.silu(gate_out) * up_out).astype(block.dtype)
        part = jnp.dot(hidden, v_down[...], preferred_element_type=jnp.float32)
        return part.astype(block.dtype).reshape(extra.shape)

    def add_up(target, sources, columns=slice(None)):
        def step(i, carry):
            at = pl.ds(pl.multiple_of(i * 16, 16), 16)
            total = sources[0][at, columns].astype(jnp.float32)
            for source in sources[1:]:
                total = total + source[at, columns].astype(jnp.float32)
            target[at, columns] = total.astype(target.dtype)
            return carry

        lax.fori_loop(0, rows // 16, step, 0)

    def serve(source, target, scale):
        block = source[...].reshape(-1, features)
        depth = w_gate.shape[0] * w_gate.shape[1]
        w_in = (w_gate[...].reshape(depth, features), w_up[...].reshape(depth, features))
        gate_out = lax.dot_general(block, w_in[0], NT, preferred_element_type=jnp.float32)
        up_out = lax.dot_general(block, w_in[1], NT, preferred_element_type=jnp.float32)
        hidden = (jax.nn.silu(gate_out) * up_out).astype(block.dtype)
        width = features // 2
        for part in (0, 1):
            result = jnp.dot(hidden, w_down[part], preferred_element_type=jnp.float32)
            result = (result * scale).astype(target.dtype)
            target[..., part * width : (part + 1) * width] = result.reshape(*target.shape[:-1], width)

    def outer(i):
        plane = planes[i]
        if i:
            block = inward.at[plane]
            arrived(block, Q_IN + plane)
            serve(block, block, worth[plane, :, 0:1])
            push(block, back.at[plane], Q_BACK + plane, q_device)
            return
        arrived(far.at[1], Q_FAR)
        serve(far, own.at[1], jnp.concatenate([factor(z, 2), factor(z, 3)], axis=0))

    def far_back():
        @pl.when(core == 0)
        def _():
            add_up(own.at[1, 0], [own.at[1, 0], extra.at[1]])

        push(own.at[1, 1], back_near.at[1], Q_BACK_FAR, q_device)
        push(own.at[1, 0], back_near.at[0], Q_BACK + z, q_device)

    def inner(i):
        plane = planes[i]
        block = held.at[plane]
        if i:
            for side in (0, 1):
                for number in leaving[i, side]:
                    left(number)
        scale = jnp.concatenate([factor(plane, 0), factor(plane, 1)], axis=0)
        serve(block, block if i else own.at[0], scale)

    half = features // 2
    columns = [pl.ds(0, half), pl.ds(half, half)]

    def spread(plane, side, part):
        places = pick[plane, :, side * rows : (side + 1) * rows]
        return lax.dot_general(
            places,
            back[plane, :, columns[part]],
            (((0,), (0,)), ((), ())),
            preferred_element_type=jnp.float32,
        )

    def q_sum(i):
        plane = planes[i]
        if i:
            block = held.at[plane, 1]
            arrived(back.at[plane], Q_BACK + plane)
            for part, at in enumerate((P_BACK, P_MORE)):
                some = block.at[:, columns[part]]
                some[...] = (some[...].astype(jnp.float32) + spread(plane, 1, part)).astype(some.dtype)
                push(some, from_p.at[plane, :, columns[part]], at + plane, p_device)
        else:
            block = own.at[0, 1]
            arrived(back_near.at[1], Q_BACK_FAR)

            @pl.when(core == 0)
            def _():
                add_up(block, [block, back_near.at[1]])

            @pl.when(core == 1)
            def _():
                add_up(block, [block, back_near.at[1], extra.at[1]])

            push(block, from_p.at[plane], P_BACK + plane, p_device)

    below, above = LINE, LINE + 1

    @pl.when(outermost)
    def _():
        from_z[0:LINE] = jnp.zeros((LINE, rows, features), from_z.dtype)

    for lacking, slot in ((0, below), (LINE - 1, above)):
        @pl.when(z == lacking)
        def _():
            from_z[slot] = jnp.zeros((rows, features), from_z.dtype)

    def p_sum(i, only=None):
        plane = planes[i]
        if i == 0:
            arrived(back_near.at[0], Q_BACK + z)
            arrived(from_p.at[plane], P_BACK + plane)
            for slot, inside in ((below, z > 0), (above, z < LINE - 1)):
                for part, at in enumerate((Z_BACK, Z_MORE)):
                    some = from_z.at[slot, :, columns[part]]
                    pl.when(inside)(lambda some=some, at=at + slot: arrived(some, at))
            sources = [own.at[0, 0], extra.at[0], back_near.at[0], from_p.at[plane]]
            add_up(out, sources + [from_z.at[below], from_z.at[above]])
            return
        to = z + jnp.where(plane < z, -1, 1)
        slot = jnp.where(to == plane, jnp.where(plane < z, above, below), plane)
        copies = []
        for part, at in enumerate((Z_BACK, Z_MORE)):
            some = held.at[plane, 0, :, columns[part]]
            target = from_z.at[slot, :, columns[part]]
            copies.append(copy_of(some, target, at + slot, len(sent), (to * 2 + x, y, core)))
            sent.append((copies[-1], only))

        def run():
            for part, at, at_z in ((0, P_BACK, Z_BACK), (1, P_MORE, Z_MORE)):
                come = from_p.at[plane, :, columns[part]]
                chain = from_z.at[plane, :, columns[part]]
                some = held.at[plane, 0, :, columns[part]]
                arrived(come, at + plane)
                pl.when(middle)(lambda chain=chain, at=at_z + plane: arrived(chain, at))
                total = some[...].astype(jnp.float32) + come[...].astype(jnp.float32)
                total = total + chain[...].astype(jnp.float32) + spread(plane, 0, part)
                some[...] = total.astype(some.dtype)
                copies[part].start()

        if only is None:
            run()
        else:
            pl.when(only)(run)

    enter(1)
    enter(2, middle)
    pass_on(0)
    for d in range(LINE):
        for side in range(4):
            if d or side:
                plane = lax.rem(z + d, LINE)
                pltpu.make_async_remote_copy(
                    src_ref=share_in.at[plane, side],
                    dst_ref=share_in.at[plane, side],
                    send_sem=share_send.at[0],
                    recv_sem=share_recv.at[plane * 4 + side],
                    device_id=q_device,
                    device_id_type=MESH,
                ).wait_recv()
    choose()
    arrived(far.at[0], Q_IN + z)
    loads[0].wait()
    pair.append(to_partner(beside, pair_in.at[1], 1))
    for copy in loads[1:4]:
        copy.wait()
    for copy in pair:
        copy.wait_recv()
    pair_out[...] = shared(pair_in[...].reshape(2 * rows, features))
    pair.append(to_partner(pair_out, pair_back, 2))
    extra[...] = shared(jnp.concatenate([held[z, 0], beside[...]], axis=0))
    enter(3, middle)
    enter(2, outermost)
    pass_on(1)
    pair[2].wait_recv()

    def combine(i, carry):
        at = pl.ds(pl.multiple_of(i * 16, 16), 16)
        for block in (0, 1):
            total = extra[block, at, :].astype(jnp.float32) + pair_back[block, at, :].astype(jnp.float32)
            extra[block, at, :] = total.astype(extra.dtype)
        return carry

    lax.fori_loop(0, rows // 16, combine, 0)
    for copy in loads[4:]:
        copy.wait()
    for copy in swaps:
        copy.wait_recv()
    outer(0)
    inner(0)
    enter(3, outermost)
    pass_on(2)
    outer(1)
    inner(1)
    pass_on(3)
    outer(2)
    outer(3)
    inner(3)
    q_sum(3)
    inner(2)
    q_sum(2)
    q_sum(1)
    far_back()
    p_sum(3)
    p_sum(1, middle)
    p_sum(2)
    p_sum(1, outermost)
    q_sum(0)
    p_sum(0)
    for number in range(len(sent)):
        left(number)
    for copy in swaps + shares + pair:
        copy.wait_send()


def dense(
    tokens,
    expert_ids,
    gate_codes,
    gate_halves,
    up_halves,
    down_halves,
    shared_gate,
    shared_up,
    shared_down,
):
    rows, features = tokens.shape
    capacity = 2 * (5 * rows * expert_ids.shape[1] // (6 * 4 * LINE) + 1)
    slots = -(-2 * capacity // 16) * 16
    half_depth = gate_halves.shape[2]
    shared_depth = shared_gate.shape[1]
    depth, width = down_halves.shape[1:]
    kind = tokens.dtype
    inside, outside = pl.BlockSpec(memory_space=pltpu.VMEM), pl.BlockSpec(memory_space=pl.ANY)
    block = (rows, features)
    dma = pltpu.SemaphoreType.DMA
    return pl.pallas_call(
        functools.partial(layer_kernel, CUT),
        out_shape=jax.ShapeDtypeStruct(block, kind),
        in_specs=[inside] * 3 + [outside] * 6,
        out_specs=inside,
        scratch_shapes=[
            pltpu.VMEM((LINE + 1, 2, *block), kind),
            pltpu.VMEM((2, 2, *block), kind),
            pltpu.VMEM((LINE, slots, features), kind),
            pltpu.VMEM((LINE, slots, features), kind),
            pltpu.VMEM((2, *block), kind),
            pltpu.VMEM((LINE, slots, features), kind),
            pltpu.VMEM((LINE, *block), kind),
            pltpu.VMEM((LINE + 2, *block), kind),
            pltpu.VMEM((2, half_depth, features), kind),
            pltpu.VMEM((2, half_depth, features), kind),
            pltpu.VMEM((2, depth, width), kind),
            pltpu.VMEM((shared_depth, features), kind),
            pltpu.VMEM((shared_depth, features), kind),
            pltpu.VMEM((shared_depth, features), kind),
            pltpu.VMEM((4 * LINE, 8, rows), jnp.float32),
            pltpu.VMEM((LINE, 4, 8, rows), jnp.float32),
            pltpu.VMEM((LINE, slots, 2 * rows), kind),
            pltpu.VMEM((LINE, slots, rows), jnp.float32),
            pltpu.VMEM((2, *block), kind),
            pltpu.VMEM((2, *block), kind),
            pltpu.VMEM((2, *block), kind),
            pltpu.VMEM((2, *block), kind),
            dma((7,)),
            dma((3,)),
            dma((3,)),
            dma((3,)),
            dma((3,)),
            dma((4 * LINE - 1,)),
            dma((4 * LINE,)),
            dma((80,)),
            dma((48,)),
        ],
        compiler_params=pltpu.CompilerParams(
            collective_id=0, has_side_effects=True, vmem_limit_bytes=62 << 20
        ),
        cost_estimate=pl.CostEstimate(flops=40 << 30, bytes_accessed=32 << 20, transcendentals=0),
    )(
        tokens,
        expert_ids.T,
        gate_codes.T,
        gate_halves[0].T,
        up_halves[0].T,
        down_halves[0],
        shared_gate.T,
        shared_up.T,
        shared_down,
    )


CUT = 2048


def program(mesh, row, pieces, body):
    in_specs = (
        P(row, None),
        P(row, None),
        P(row, None),
        P(row, None, None),
        P(row, None, None),
        P(row, None, None),
        P(None, pieces),
        P(None, pieces),
        P(pieces, None),
    )
    return jax.shard_map(
        body, mesh=mesh, in_specs=in_specs, out_specs=P(row, None), check_vma=False
    )


def solution(mesh):
    fine = jax.sharding.Mesh(
        mesh.devices.reshape(mesh.devices.shape[0], -1, 2), ("node", "chip", "core")
    )

    def run(tokens, expert_ids, *others):
        if mesh.shape["local"] == 4 and mesh.shape["node"] == 2 * LINE:
            whole = program(fine, ("node", "chip", "core"), ("chip", "core"), dense)
        else:
            whole = program(mesh, ("node", "local"), "local", local)
        return whole(tokens, expert_ids, *others)

    return run
```

```python
import functools

import jax
import jax.numpy as jnp
from jax import lax
from jax.experimental import pallas as pl
from jax.experimental.pallas import tpu as pltpu
from jax.sharding import PartitionSpec as P

MESH = pl.DeviceIdType.MESH
NT = (((1,), (1,)), ((), ()))


def from_partner(block, axis, distance):
    count = lax.axis_size(axis)
    route = []
    for low in range(count):
        high = low | 1 << distance
        if high != low and high < count:
            route += [(low, high), (high, low)]
    return lax.ppermute(block, axis, route)


def dispatch(send_block):
    return lax.all_to_all(send_block, ("node", "local"), split_axis=0, concat_axis=0, tiled=True)


def combine(send_block):
    return lax.all_to_all(send_block, ("node", "local"), split_axis=0, concat_axis=0, tiled=True)


def half_hidden(received, gate_half, up_half, dtype):
    expert_rows = received.reshape(-1, received.shape[-1])
    gate_out = jnp.dot(expert_rows, gate_half, preferred_element_type=jnp.float32)
    up_out = jnp.dot(expert_rows, up_half, preferred_element_type=jnp.float32)
    return (jax.nn.silu(gate_out) * up_out).astype(dtype)


def side_by_side(own_part, other_part, parity, axis):
    lower = jnp.where(parity == 0, own_part, other_part)
    upper = jnp.where(parity == 0, other_part, own_part)
    return jnp.concatenate([lower, upper], axis=axis)


def local(
    tokens,
    expert_ids,
    gate_codes,
    gate_halves,
    up_halves,
    down_halves,
    shared_gate,
    shared_up,
    shared_down,
):
    tok_rows, features = tokens.shape
    fanout = expert_ids.shape[1]
    devices = lax.axis_size("node") * lax.axis_size("local")
    experts = devices // 2
    capacity = 2 * (5 * tok_rows * fanout // (6 * experts) + 1)
    parity = lax.axis_index("local") % 2
    flat_ids = expert_ids.reshape(-1)
    onehot = (flat_ids[:, None] == jnp.arange(experts, dtype=jnp.int32)[None, :]).astype(jnp.int32)
    order = jnp.arange(flat_ids.shape[0], dtype=jnp.int32)
    earlier = (order[:, None] > order[None, :]).astype(jnp.bfloat16)
    before = jnp.dot(earlier, onehot.astype(jnp.bfloat16), preferred_element_type=jnp.float32)
    slot_index = jnp.sum(before.astype(jnp.int32) * onehot, axis=1)
    dest_row = flat_ids * capacity + slot_index
    owner_row = jnp.arange(tok_rows * fanout, dtype=jnp.int32) // fanout
    buffer = (
        jnp.zeros((experts * capacity, features), tokens.dtype).at[dest_row].set(tokens[owner_row])
    )
    codes = gate_codes.astype(jnp.float32)
    weights = (codes / jnp.sum(codes, axis=1, keepdims=True)).reshape(-1)
    send_block = jnp.broadcast_to(
        buffer.reshape(experts, 1, capacity, features), (experts, 2, capacity, features)
    ).reshape(devices, capacity, features)
    received = dispatch(send_block)
    hidden_own = half_hidden(received, gate_halves[0], up_halves[0], tokens.dtype)
    hidden_other = from_partner(hidden_own, "local", 0)
    hidden = side_by_side(hidden_own, hidden_other, parity, 1)
    result = jnp.dot(hidden, down_halves[0], preferred_element_type=jnp.float32).astype(
        tokens.dtype
    )
    returned = combine(result.reshape(devices, capacity, features // 2))
    outputs = (
        returned.reshape(experts, 2, capacity, features // 2)
        .transpose(0, 2, 1, 3)
        .reshape(experts * capacity, features)
    )
    picked = outputs[dest_row].astype(jnp.float32) * weights[:, None]
    routed = jnp.sum(picked.reshape(tok_rows, fanout, features), axis=1)
    block_rows = lax.all_gather(tokens, "local", axis=0, tiled=True)
    gate_part = jnp.dot(block_rows, shared_gate, preferred_element_type=jnp.float32)
    up_part = jnp.dot(block_rows, shared_up, preferred_element_type=jnp.float32)
    shared_hidden = (jax.nn.silu(gate_part) * up_part).astype(tokens.dtype)
    block_rows = shared_hidden
    shared_out = lax.psum_scatter(
        jnp.dot(block_rows, shared_down, preferred_element_type=jnp.float32).astype(jnp.bfloat16),
        "local",
        scatter_dimension=0,
        tiled=True,
    ).astype(jnp.float32)
    return (routed + shared_out).astype(tokens.dtype)


LINE = 4


def layer_kernel(cut, *refs):
    tokens, ids, codes, gate, up, down, s_gate, s_up, s_down, out = refs[:10]
    held, own, inward, outward, back_near, back, from_p, from_z = refs[10:18]
    w_gate, w_up, w_down, v_gate, v_up, v_down = refs[18:24]
    tab, pick, pair_in, pair_out, pair_back, extra = refs[24:30]
    load_sem, swap_send, swap_recv, pair_send, pair_recv = refs[30:35]
    send_sem, recv_sem = refs[35:]
    rows, features = tokens.shape
    node, y, core = lax.axis_index("node"), lax.axis_index("chip"), lax.axis_index("core")
    z, x = node // 2, node % 2
    upper = z // 2
    planes = [z, z + 1 - 2 * (z % 2), 2 - upper, 3 - 3 * upper]
    slots = inward.shape[1]
    beside = held.at[LINE * (1 - core) + z * core, core]
    far = held.at[LINE]

    def spot(plane, side):
        flip_x = (side % 2) * (1 - core) + (side // 2) * core
        flip_y = (side % 2) * core + (side // 2) * (1 - core)
        return plane, x + flip_x * (1 - 2 * x), y + flip_y * (1 - 2 * y)

    def device(plane, side):
        at_z, at_x, at_y = spot(plane, side)
        return at_z * 2 + at_x, at_y, core

    partner = (node, y, 1 - core)
    p_device, q_device = device(z, 1), device(z, 2)
    mine = node * 2 + y
    beyond = jnp.where(core == 0, node * 2 + 1 - y, (z * 2 + 1 - x) * 2 + y)
    barrier = pltpu.get_barrier_semaphore()
    for target in (p_device, q_device, partner):
        pl.semaphore_signal(barrier, inc=1, device_id=target, device_id_type=MESH)
    for to in (z - 1, z + 1):

        @pl.when(jnp.logical_and(to >= 0, to < LINE))
        def _():
            pl.semaphore_signal(barrier, inc=1, device_id=(to * 2 + x, y, core), device_id_type=MESH)

    peers = 4 + jnp.where(jnp.logical_and(z > 0, z < LINE - 1), 1, 0)
    pl.semaphore_wait(barrier, peers)

    Z_WHOLE, Z_REST, P_IN, Q_IN, Q_BACK, P_BACK, P_MORE, Z_BACK = (LINE * k for k in range(8))
    Z_MORE = Z_BACK + LINE + 2
    Q_FAR, Q_BACK_FAR, T_FAR = (Z_MORE + LINE + 2 + k for k in range(3))
    T_Z, T_P, T_Q = (T_FAR + 1 + LINE * k for k in range(3))
    middle = jnp.logical_and(z > 0, z < LINE - 1)
    outermost = jnp.logical_not(middle)
    sent = []

    def copy_of(source, target, at, number, to):
        return pltpu.make_async_remote_copy(
            src_ref=source,
            dst_ref=target,
            send_sem=send_sem.at[number],
            recv_sem=recv_sem.at[at],
            device_id=to,
            device_id_type=MESH,
        )

    def push(source, target, at, to, allowed=None):
        copy = copy_of(source, target, at, len(sent), to)
        if allowed is None:
            copy.start()
        else:
            pl.when(allowed)(copy.start)
        sent.append((copy, allowed))
        return len(sent) - 1

    waited = set()

    def left(number):
        if number in waited:
            return
        waited.add(number)
        copy, allowed = sent[number]
        if allowed is None:
            copy.wait_send()
        else:
            pl.when(allowed)(copy.wait_send)

    def arrived(target, at):
        copy_of(target, target, at, 0, q_device).wait_recv()

    def first(ref):
        return ref.at[:, pl.ds(0, cut)]

    def rest(ref):
        return ref.at[:, pl.ds(cut, features - cut)]

    leaving = {(i, side): [] for i in range(LINE) for side in (0, 1, 2)}

    def along_z(source, target, at, i, side, only=None):
        if i == 0:
            for step in (1, -1):
                to = z + step
                inside = jnp.logical_and(to >= 0, to < LINE)
                to = jnp.clip(to, 0, LINE - 1)
                leaving[i, side].append(push(source, target, at, (to * 2 + x, y, core), inside))
        else:
            to = z + jnp.where(planes[i] < z, 1, -1)
            inside = jnp.logical_and(to >= 0, to < LINE)
            if only is not None:
                inside = jnp.logical_and(inside, only)
            to = jnp.clip(to, 0, LINE - 1)
            leaving[i, side].append(push(source, target, at, (to * 2 + x, y, core), inside))

    push(tokens, far.at[0], Q_IN + z, q_device)
    push(tokens, held.at[z, 1], P_IN + z, p_device)
    along_z(tokens, held.at[z, 0], Z_WHOLE + z, 0, 0)

    def to_partner(source, target, at):
        copy = pltpu.make_async_remote_copy(
            src_ref=source,
            dst_ref=target,
            send_sem=pair_send.at[at],
            recv_sem=pair_recv.at[at],
            device_id=partner,
            device_id_type=MESH,
        )
        copy.start()
        return copy

    pair = [to_partner(tokens, pair_in.at[0], 0)]
    swaps = []
    for at, (source, target) in enumerate(((gate, w_gate), (up, w_up), (down, w_down))):
        copy = pltpu.make_async_remote_copy(
            src_ref=source,
            dst_ref=target.at[core],
            send_sem=swap_send.at[at],
            recv_sem=swap_recv.at[at],
            device_id=partner,
            device_id_type=MESH,
        )
        copy.start()
        swaps.append(copy)
    loads = [
        pltpu.make_async_copy(source, target, load_sem.at[at])
        for at, (source, target) in enumerate(
            (
                (tokens, held.at[z, 0]),
                (s_gate, v_gate),
                (s_up, v_up),
                (s_down, v_down),
                (gate, w_gate.at[core]),
                (up, w_up.at[core]),
                (down, w_down.at[core]),
            )
        )
    ]
    for copy in loads:
        copy.start()

    scores = codes[...].astype(jnp.float32)
    scores = scores / jnp.sum(scores, axis=0, keepdims=True)
    names = lax.broadcasted_iota(jnp.int32, (4 * LINE, rows), 0)
    table = jnp.zeros((4 * LINE, rows), jnp.float32)
    for k in range(ids.shape[0]):
        table = table + jnp.where(ids[k : k + 1, :] == names, scores[k : k + 1, :], 0.0)
    tab[z, 0] = table
    push(tab.at[z, 0], tab.at[z, 2], T_Q + z, q_device)
    push(tab.at[z, 0], tab.at[z, 1], T_P + z, p_device)
    along_z(tab.at[z, 0], tab.at[z, 0], T_Z + z, 0, 2)

    def row(plane, side, expert):
        return tab[plane, side, pl.ds(expert, 1), :]

    def factor(plane, side):
        return jnp.broadcast_to(row(plane, side, mine), (rows, rows)).T[:, 0:1]

    square = (2 * rows, 2 * rows)
    earlier = lax.broadcasted_iota(jnp.int32, square, 0) < lax.broadcasted_iota(jnp.int32, square, 1)
    earlier = jnp.where(earlier, 1.0, 0.0).astype(jnp.bfloat16)
    slot_row = lax.broadcasted_iota(jnp.int32, (slots, 2 * rows), 0).astype(jnp.float32)

    def slotted(plane, sides, expert, values):
        listed = jnp.concatenate([row(plane, side, expert) for side in sides], axis=1)
        named = jnp.broadcast_to(jnp.where(listed > 0, 1.0, 0.0), (16, 2 * rows)).astype(jnp.bfloat16)
        rank = jnp.dot(named, earlier, preferred_element_type=jnp.float32)[0:1]
        rank = jnp.where(listed > 0, rank, -1.0)
        return jnp.where(rank == slot_row, listed if values else 1.0, 0.0)

    def enter(i, only=None):
        plane = planes[i]
        block = held.at[plane, 0]
        if only is None:
            arrived(block, Z_WHOLE + plane)
        else:
            pl.when(only)(lambda: arrived(block, Z_WHOLE + plane))
        listed = tab.at[plane, 0]
        if only is None:
            arrived(listed, T_Z + plane)
        else:
            pl.when(only)(lambda: arrived(listed, T_Z + plane))
        along_z(listed, listed, T_Z + plane, i, 2, only)
        push(listed, tab.at[plane, 1], T_P + plane, p_device, only)
        along_z(block, block, Z_WHOLE + plane, i, 0, only)
        target = held.at[plane, 1]
        leaving[i, 0].append(push(first(block), first(target), P_IN + plane, p_device, only))

    def pass_on(i):
        plane = planes[i]
        block = held.at[plane, 1]
        if i == 0 or cut == features:
            arrived(block, P_IN + plane)
        else:
            arrived(first(block), P_IN + plane)
            arrived(rest(block), Z_REST + plane)
        if cut < features:
            along_z(rest(block), rest(block), Z_REST + plane, i, 1)
        arrived(tab.at[plane, 1], T_P + plane)
        if i == 0:
            leaving[i, 1].append(push(block, far.at[1], Q_FAR, q_device))
            push(tab.at[plane, 1], tab.at[plane, 3], T_FAR, q_device)
        else:
            push(tab.at[plane, pl.ds(0, 2)], tab.at[plane, pl.ds(2, 2)], T_Q + plane, q_device)
            pick[plane] = slotted(plane, (0, 1), beyond, False).astype(pick.dtype)
            both = held[plane].reshape(2 * rows, features)
            chosen = jnp.dot(pick[plane], both, preferred_element_type=jnp.float32)
            outward[plane] = chosen.astype(outward.dtype)
            push(outward.at[plane], inward.at[plane], Q_IN + plane, q_device)

    def shared(block):
        gate_out = lax.dot_general(block, v_gate[...], NT, preferred_element_type=jnp.float32)
        up_out = lax.dot_general(block, v_up[...], NT, preferred_element_type=jnp.float32)
        hidden = (jax.nn.silu(gate_out) * up_out).astype(block.dtype)
        part = jnp.dot(hidden, v_down[...], preferred_element_type=jnp.float32)
        return part.astype(block.dtype).reshape(extra.shape)

    def add_up(target, sources, columns=slice(None)):
        def step(i, carry):
            at = pl.ds(pl.multiple_of(i * 16, 16), 16)
            total = sources[0][at, columns].astype(jnp.float32)
            for source in sources[1:]:
                total = total + source[at, columns].astype(jnp.float32)
            target[at, columns] = total.astype(target.dtype)
            return carry

        lax.fori_loop(0, rows // 16, step, 0)

    def serve(source, target, scale):
        block = source[...].reshape(-1, features)
        depth = w_gate.shape[0] * w_gate.shape[1]
        w_in = (w_gate[...].reshape(depth, features), w_up[...].reshape(depth, features))
        gate_out = lax.dot_general(block, w_in[0], NT, preferred_element_type=jnp.float32)
        up_out = lax.dot_general(block, w_in[1], NT, preferred_element_type=jnp.float32)
        hidden = (jax.nn.silu(gate_out) * up_out).astype(block.dtype)
        width = features // 2
        for part in (0, 1):
            result = jnp.dot(hidden, w_down[part], preferred_element_type=jnp.float32)
            result = (result * scale).astype(target.dtype)
            target[..., part * width : (part + 1) * width] = result.reshape(*target.shape[:-1], width)

    def outer(i):
        plane = planes[i]
        if i:
            block = inward.at[plane]
            arrived(block, Q_IN + plane)
            arrived(tab.at[plane, pl.ds(2, 2)], T_Q + plane)
            worth = jnp.sum(slotted(plane, (2, 3), mine, True), axis=1, keepdims=True)
            serve(block, block, worth)
            push(block, back.at[plane], Q_BACK + plane, q_device)
            return
        arrived(far.at[1], Q_FAR)
        arrived(tab.at[plane, 2], T_Q + plane)
        arrived(tab.at[plane, 3], T_FAR)
        serve(far, own.at[1], jnp.concatenate([factor(z, 2), factor(z, 3)], axis=0))

    def far_back():
        @pl.when(core == 0)
        def _():
            add_up(own.at[1, 0], [own.at[1, 0], extra.at[1]])

        push(own.at[1, 1], back_near.at[1], Q_BACK_FAR, q_device)
        push(own.at[1, 0], back_near.at[0], Q_BACK + z, q_device)

    def inner(i):
        plane = planes[i]
        block = held.at[plane]
        if i:
            for side in (0, 1):
                for number in leaving[i, side]:
                    left(number)
        scale = jnp.concatenate([factor(plane, 0), factor(plane, 1)], axis=0)
        serve(block, block if i else own.at[0], scale)

    half = features // 2
    columns = [pl.ds(0, half), pl.ds(half, half)]

    def spread(plane, side, part):
        places = pick[plane, :, side * rows : (side + 1) * rows]
        return lax.dot_general(
            places,
            back[plane, :, columns[part]],
            (((0,), (0,)), ((), ())),
            preferred_element_type=jnp.float32,
        )

    def q_sum(i):
        plane = planes[i]
        if i:
            block = held.at[plane, 1]
            arrived(back.at[plane], Q_BACK + plane)
            for part, at in enumerate((P_BACK, P_MORE)):
                some = block.at[:, columns[part]]
                some[...] = (some[...].astype(jnp.float32) + spread(plane, 1, part)).astype(some.dtype)
                push(some, from_p.at[plane, :, columns[part]], at + plane, p_device)
        else:
            block = own.at[0, 1]
            arrived(back_near.at[1], Q_BACK_FAR)

            @pl.when(core == 0)
            def _():
                add_up(block, [block, back_near.at[1]])

            @pl.when(core == 1)
            def _():
                add_up(block, [block, back_near.at[1], extra.at[1]])

            push(block, from_p.at[plane], P_BACK + plane, p_device)

    below, above = LINE, LINE + 1

    @pl.when(outermost)
    def _():
        from_z[0:LINE] = jnp.zeros((LINE, rows, features), from_z.dtype)

    for lacking, slot in ((0, below), (LINE - 1, above)):
        @pl.when(z == lacking)
        def _():
            from_z[slot] = jnp.zeros((rows, features), from_z.dtype)

    def p_sum(i, only=None):
        plane = planes[i]
        if i == 0:
            arrived(back_near.at[0], Q_BACK + z)
            arrived(from_p.at[plane], P_BACK + plane)
            for slot, inside in ((below, z > 0), (above, z < LINE - 1)):
                for part, at in enumerate((Z_BACK, Z_MORE)):
                    some = from_z.at[slot, :, columns[part]]
                    pl.when(inside)(lambda some=some, at=at + slot: arrived(some, at))
            sources = [own.at[0, 0], extra.at[0], back_near.at[0], from_p.at[plane]]
            add_up(out, sources + [from_z.at[below], from_z.at[above]])
            return
        to = z + jnp.where(plane < z, -1, 1)
        slot = jnp.where(to == plane, jnp.where(plane < z, above, below), plane)
        copies = []
        for part, at in enumerate((Z_BACK, Z_MORE)):
            some = held.at[plane, 0, :, columns[part]]
            target = from_z.at[slot, :, columns[part]]
            copies.append(copy_of(some, target, at + slot, len(sent), (to * 2 + x, y, core)))
            sent.append((copies[-1], only))

        def run():
            for part, at, at_z in ((0, P_BACK, Z_BACK), (1, P_MORE, Z_MORE)):
                come = from_p.at[plane, :, columns[part]]
                chain = from_z.at[plane, :, columns[part]]
                some = held.at[plane, 0, :, columns[part]]
                arrived(come, at + plane)
                pl.when(middle)(lambda chain=chain, at=at_z + plane: arrived(chain, at))
                total = some[...].astype(jnp.float32) + come[...].astype(jnp.float32)
                total = total + chain[...].astype(jnp.float32) + spread(plane, 0, part)
                some[...] = total.astype(some.dtype)
                copies[part].start()

        if only is None:
            run()
        else:
            pl.when(only)(run)

    enter(1)
    enter(2, middle)
    pass_on(0)
    arrived(far.at[0], Q_IN + z)
    loads[0].wait()
    pair.append(to_partner(beside, pair_in.at[1], 1))
    for copy in loads[1:4]:
        copy.wait()
    for copy in pair:
        copy.wait_recv()
    pair_out[...] = shared(pair_in[...].reshape(2 * rows, features))
    pair.append(to_partner(pair_out, pair_back, 2))
    extra[...] = shared(jnp.concatenate([held[z, 0], beside[...]], axis=0))
    enter(3, middle)
    enter(2, outermost)
    pass_on(1)
    pair[2].wait_recv()

    def combine(i, carry):
        at = pl.ds(pl.multiple_of(i * 16, 16), 16)
        for block in (0, 1):
            total = extra[block, at, :].astype(jnp.float32) + pair_back[block, at, :].astype(jnp.float32)
            extra[block, at, :] = total.astype(extra.dtype)
        return carry

    lax.fori_loop(0, rows // 16, combine, 0)
    for copy in loads[4:]:
        copy.wait()
    for copy in swaps:
        copy.wait_recv()
    outer(0)
    inner(0)
    enter(3, outermost)
    pass_on(2)
    outer(1)
    inner(1)
    pass_on(3)
    outer(2)
    outer(3)
    inner(3)
    q_sum(3)
    inner(2)
    q_sum(2)
    q_sum(1)
    far_back()
    p_sum(3)
    p_sum(1, middle)
    p_sum(2)
    p_sum(1, outermost)
    q_sum(0)
    p_sum(0)
    for number in range(len(sent)):
        left(number)
    for copy in swaps + pair:
        copy.wait_send()


def dense(
    tokens,
    expert_ids,
    gate_codes,
    gate_halves,
    up_halves,
    down_halves,
    shared_gate,
    shared_up,
    shared_down,
):
    rows, features = tokens.shape
    capacity = 2 * (5 * rows * expert_ids.shape[1] // (6 * 4 * LINE) + 1)
    slots = -(-2 * capacity // 16) * 16
    half_depth = gate_halves.shape[2]
    shared_depth = shared_gate.shape[1]
    depth, width = down_halves.shape[1:]
    kind = tokens.dtype
    inside, outside = pl.BlockSpec(memory_space=pltpu.VMEM), pl.BlockSpec(memory_space=pl.ANY)
    block = (rows, features)
    dma = pltpu.SemaphoreType.DMA
    return pl.pallas_call(
        functools.partial(layer_kernel, CUT),
        out_shape=jax.ShapeDtypeStruct(block, kind),
        in_specs=[inside] * 3 + [outside] * 6,
        out_specs=inside,
        scratch_shapes=[
            pltpu.VMEM((LINE + 1, 2, *block), kind),
            pltpu.VMEM((2, 2, *block), kind),
            pltpu.VMEM((LINE, slots, features), kind),
            pltpu.VMEM((LINE, slots, features), kind),
            pltpu.VMEM((2, *block), kind),
            pltpu.VMEM((LINE, slots, features), kind),
            pltpu.VMEM((LINE, *block), kind),
            pltpu.VMEM((LINE + 2, *block), kind),
            pltpu.VMEM((2, half_depth, features), kind),
            pltpu.VMEM((2, half_depth, features), kind),
            pltpu.VMEM((2, depth, width), kind),
            pltpu.VMEM((shared_depth, features), kind),
            pltpu.VMEM((shared_depth, features), kind),
            pltpu.VMEM((shared_depth, features), kind),
            pltpu.VMEM((LINE, 4, 4 * LINE, rows), jnp.float32),
            pltpu.VMEM((LINE, slots, 2 * rows), kind),
            pltpu.VMEM((2, *block), kind),
            pltpu.VMEM((2, *block), kind),
            pltpu.VMEM((2, *block), kind),
            pltpu.VMEM((2, *block), kind),
            dma((7,)),
            dma((3,)),
            dma((3,)),
            dma((3,)),
            dma((3,)),
            dma((112,)),
            dma((64,)),
        ],
        compiler_params=pltpu.CompilerParams(
            collective_id=0, has_side_effects=True, vmem_limit_bytes=62 << 20
        ),
        cost_estimate=pl.CostEstimate(flops=40 << 30, bytes_accessed=32 << 20, transcendentals=0),
    )(
        tokens,
        expert_ids.T,
        gate_codes.T,
        gate_halves[0].T,
        up_halves[0].T,
        down_halves[0],
        shared_gate.T,
        shared_up.T,
        shared_down,
    )


CUT = 2048


def program(mesh, row, pieces, body):
    in_specs = (
        P(row, None),
        P(row, None),
        P(row, None),
        P(row, None, None),
        P(row, None, None),
        P(row, None, None),
        P(None, pieces),
        P(None, pieces),
        P(pieces, None),
    )
    return jax.shard_map(
        body, mesh=mesh, in_specs=in_specs, out_specs=P(row, None), check_vma=False
    )


def solution(mesh):
    fine = jax.sharding.Mesh(
        mesh.devices.reshape(mesh.devices.shape[0], -1, 2), ("node", "chip", "core")
    )

    def run(tokens, expert_ids, *others):
        if mesh.shape["local"] == 4 and mesh.shape["node"] == 2 * LINE:
            whole = program(fine, ("node", "chip", "core"), ("chip", "core"), dense)
        else:
            whole = program(mesh, ("node", "local"), "local", local)
        return whole(tokens, expert_ids, *others)

    return run
```
